32 devices in a mesh: dp: 2 (over y), tile: 4 (over z), replica: 4 (over x, core).
Axes of the slice: x: 2, y: 2, z: 4, core: 2. Of those that a mesh axis runs over, the one named last changes fastest.
Arguments:
- tokens: bfloat16 [128, 8192], P(('tile', 'replica'), 'dp'), may hold values from -6 to 6
- out_grad: bfloat16 [128, 8192], P(('tile', 'replica'), 'dp'), may hold values from -3 to 3
- gate_blocks: bfloat16 [2, 4, 384, 128, 128], P('dp', 'tile'), may hold values from -0.125 to 0.125
- up_blocks: bfloat16 [2, 4, 384, 128, 128], P('dp', 'tile'), may hold values from -0.125 to 0.125
- down_blocks: bfloat16 [2, 4, 384, 128, 128], P('dp', 'tile'), may hold values from -0.09375 to 0.09375
- gate_ids: int32 [2, 4, 384], P('dp', 'tile'), may hold values from 0 to 896, as said below
- up_ids: int32 [2, 4, 384], P('dp', 'tile'), may hold values from 0 to 896, as said below
- down_ids: int32 [2, 4, 384], P('dp', 'tile'), may hold values from 0 to 896, as said below
Outputs:
- output: bfloat16 [128, 8192], P(('tile', 'replica'), 'dp')
- input_grad: bfloat16 [128, 8192], P(('tile', 'replica'), 'dp')
- gate_grad: bfloat16 [2, 4, 384, 128, 128], P('dp', 'tile')
- up_grad: bfloat16 [2, 4, 384, 128, 128], P('dp', 'tile')
- down_grad: bfloat16 [2, 4, 384, 128, 128], P('dp', 'tile')
The draws below stay inside these ranges and needn't reach their ends.
Inputs may be any that keep to these rules, and one draw needn't show every extreme that they name: `gate_ids`: entry s for device (d, t) names a kept block of its 32 x 28 grid as row * 28 + column, each block at most once for a device; the value 896 marks an empty slot. Every device keeps 64 to 384 blocks; in every draw some device fills all 384 slots and another keeps 64 blocks. `up_ids`: as for gate_ids, drawn apart. `down_ids`: as for gate_ids, drawn apart; the row names a model-width block, the column a hidden-unit block.
All inputs are finite; a program needn't handle non-finite values.
Results may differ from the reference program's by a relative error of at most 0.017.
Values may be sent and summed in bfloat16 or wider, within the bound.
No kernel may reach another device: no remote copies, remote signals or barrier semaphores. Data moves between devices by JAX's collectives and lax.ppermute only.
A program may use at most 256 MiB of HBM per device.

```python
import jax
import jax.numpy as jnp
from jax import lax

D = 8192
FF = 14336
BLK = 128
TOK_DEV = 8
TOKENS = 128
RB_DEV = 32
CB_DEV = 28
GRID = 896
SLOTS = 384
N_DP = 2
N_TILE = 4
N_REPLICA = 4


def permute_grid(subkey):
    return jax.random.permutation(subkey, GRID)


def block_ids(key):
    devices = N_DP * N_TILE
    count_key, full_key, order_key = jax.random.split(key, 3)
    fewest = max(GRID // 2 - SLOTS, 0)
    counts = jax.random.randint(count_key, (devices,), fewest, SLOTS + 1)
    fullest = jax.random.randint(full_key, (), 0, devices)
    position = jnp.arange(devices)
    counts = jnp.where(position == fullest, SLOTS, counts)
    counts = jnp.where(position == (fullest + 1) % devices, fewest, counts)
    order_keys = jax.random.split(order_key, devices)
    orders = jax.vmap(permute_grid)(order_keys)[:, :SLOTS]
    slot_index = jnp.arange(SLOTS)[None, :]
    chosen = jnp.where(slot_index < counts[:, None], orders, GRID)
    return chosen.reshape(N_DP, N_TILE, SLOTS).astype(jnp.int32)


def draw_gate_ids(key, part):
    return block_ids(jax.random.fold_in(key, 11))


def draw_up_ids(key, part):
    return block_ids(jax.random.fold_in(key, 23))


def draw_down_ids(key, part):
    return block_ids(jax.random.fold_in(key, 37))


def level_of(own_key, shape, shards, least, top_value):
    factor_of, own = 1.0, jax.random.fold_in(own_key, 6)
    for dim, shards_of in shards:
        heights = jnp.exp(jax.random.uniform(jax.random.fold_in(own, dim), (shards_of,), jnp.float32, least / len(shards), top_value / len(shards)))
        factor_of = factor_of * jnp.repeat(heights, shape[dim] // shards_of).reshape([-1 if axis == dim else 1 for axis in range(len(shape))])
    return factor_of


def gaussian(rng, shape, width, limit, cuts=(), kind=jnp.bfloat16):
    level = level_of(rng, shape, cuts, -0.22, 0.18) if cuts else 1.0
    array = jax.random.normal(rng, shape, jnp.float32) * width * level
    return jnp.minimum(jnp.maximum(array, -limit), limit).astype(kind)


def setup_inputs(seed: int = 0) -> dict:
    keys = jax.random.split(jax.random.key(seed), 9)
    return {
        "tokens": gaussian(keys[0], (TOKENS, D), 1.0, 6.0, ((0, 16), (1, 2))),
        "out_grad": gaussian(keys[1], (TOKENS, D), 0.5, 3.0, ((0, 16), (1, 2))),
        "gate_blocks": gaussian(keys[2], (N_DP, N_TILE, SLOTS, BLK, BLK), (D // 4) ** -0.5, 0.125, ((0, 2), (1, 4))),
        "up_blocks": gaussian(keys[3], (N_DP, N_TILE, SLOTS, BLK, BLK), (D // 4) ** -0.5, 0.125, ((0, 2), (1, 4))),
        "down_blocks": gaussian(keys[4], (N_DP, N_TILE, SLOTS, BLK, BLK), (FF // 4) ** -0.5, 0.09375, ((0, 2), (1, 4))),
        "gate_ids": draw_gate_ids(jax.random.fold_in(keys[8], 71), 0),
        "up_ids": draw_up_ids(jax.random.fold_in(keys[8], 71), 0),
        "down_ids": draw_down_ids(jax.random.fold_in(keys[8], 71), 0),
    }


def block_masks(slot_ids, row_count, col_count):
    present = slot_ids < row_count * col_count
    row_index = slot_ids // col_count
    col_index = slot_ids % col_count
    row_hot = (row_index[:, None] == jnp.arange(row_count)[None, :]) & present[:, None]
    col_hot = (col_index[:, None] == jnp.arange(col_count)[None, :]) & present[:, None]
    return (row_hot.astype(jnp.float32), col_hot.astype(jnp.float32))

def select_blocks(matrix, hot):
    blocked = matrix.astype(jnp.float32).reshape(matrix.shape[0], hot.shape[1], BLK)
    picked = jnp.einsum('tbk,sb->tsk', blocked, hot, precision=lax.Precision.HIGHEST)
    return picked.astype(jnp.bfloat16)

def place_blocks(product, hot):
    placed = jnp.einsum('tsk,sb->tbk', product, hot, precision=lax.Precision.HIGHEST)
    return placed.reshape(product.shape[0], hot.shape[1] * BLK)

def rounded(term_value):
    return lax.optimization_barrier(term_value.astype(jnp.bfloat16)).astype(jnp.float32)

def gate_forward(model_part, hidden_part, blocks, slot_ids):
    row_hot, col_hot = block_masks(slot_ids, RB_DEV, CB_DEV)
    picked = select_blocks(model_part, row_hot).astype(jnp.float32)
    product = jnp.einsum('tsk,skf->tsf', picked, blocks.astype(jnp.float32))
    return place_blocks(product, col_hot)

def down_forward(model_part, hidden_part, blocks, slot_ids):
    row_hot, col_hot = block_masks(slot_ids, RB_DEV, CB_DEV)
    picked = select_blocks(hidden_part, col_hot).astype(jnp.float32)
    product = jnp.einsum('tsf,sfk->tsk', picked, blocks.astype(jnp.float32))
    return place_blocks(product, row_hot)

def down_backward(model_part, hidden_part, blocks, slot_ids):
    row_hot, col_hot = block_masks(slot_ids, RB_DEV, CB_DEV)
    picked = select_blocks(model_part, row_hot).astype(jnp.float32)
    product = jnp.einsum('tsk,sfk->tsf', picked, blocks.astype(jnp.float32))
    return place_blocks(product, col_hot)

def gate_backward(model_part, hidden_part, blocks, slot_ids):
    row_hot, col_hot = block_masks(slot_ids, RB_DEV, CB_DEV)
    picked = select_blocks(hidden_part, col_hot).astype(jnp.float32)
    product = jnp.einsum('tsf,skf->tsk', picked, blocks.astype(jnp.float32))
    return place_blocks(product, row_hot)

def gate_weight_grad(model_part, hidden_part, blocks, slot_ids):
    row_hot, col_hot = block_masks(slot_ids, RB_DEV, CB_DEV)
    model_picked = select_blocks(model_part, row_hot).astype(jnp.float32)
    hidden_picked = select_blocks(hidden_part, col_hot).astype(jnp.float32)
    return jnp.einsum('tsk,tsf->skf', model_picked, hidden_picked)

def down_weight_grad(model_part, hidden_part, blocks, slot_ids):
    row_hot, col_hot = block_masks(slot_ids, RB_DEV, CB_DEV)
    model_picked = select_blocks(model_part, row_hot).astype(jnp.float32)
    hidden_picked = select_blocks(hidden_part, col_hot).astype(jnp.float32)
    return jnp.einsum('tsf,tsk->sfk', hidden_picked, model_picked)

def over_devices(function, by_row, by_col, blocks, slot_ids):

    def one_row(row_args):
        row_value, row_blocks, row_ids = row_args
        return jax.vmap(lambda col_value, col_blocks, col_ids: function(row_value, col_value, col_blocks, col_ids))(by_col, row_blocks, row_ids)
    return lax.map(one_row, (by_row, blocks, slot_ids))

def reference(tokens, out_grad, gate_blocks, up_blocks, down_blocks, gate_ids, up_ids, down_ids):
    group_rows = N_TILE * TOK_DEV
    width_dev = D // N_DP
    hidden_dev = FF // N_TILE

    def regroup(matrix):
        return matrix.reshape(N_TILE, N_REPLICA, TOK_DEV, D).transpose(1, 0, 2, 3).reshape(N_REPLICA, group_rows, D)

    def ungroup(stacked):
        return stacked.reshape(N_REPLICA, N_TILE, TOK_DEV, D).transpose(1, 0, 2, 3).reshape(TOKENS, D)

    def by_model(matrix):
        return matrix.reshape(group_rows, N_DP, width_dev).transpose(1, 0, 2)

    def by_hidden(matrix):
        return matrix.reshape(group_rows, N_TILE, hidden_dev).transpose(1, 0, 2)

    def hidden_whole(parts):
        return parts.transpose(1, 0, 2).reshape(group_rows, FF)

    def model_whole(parts):
        return parts.transpose(1, 0, 2).reshape(group_rows, D)
    placeholder = jnp.zeros((N_TILE, 1), jnp.float32)
    token_groups = regroup(tokens)
    grad_groups = regroup(out_grad)
    outputs = []
    input_grads = []
    gate_total = jnp.zeros(gate_blocks.shape, jnp.float32)
    up_total = jnp.zeros(up_blocks.shape, jnp.float32)
    down_total = jnp.zeros(down_blocks.shape, jnp.float32)
    for group_index in range(N_REPLICA):
        model_in = by_model(token_groups[group_index])
        model_grad = by_model(grad_groups[group_index])
        gate_parts = over_devices(gate_forward, model_in, placeholder, gate_blocks, gate_ids)
        up_parts = over_devices(gate_forward, model_in, placeholder, up_blocks, up_ids)
        gate_sum = hidden_whole(lax.optimization_barrier(jnp.sum(rounded(gate_parts), axis=0)))
        up_sum = hidden_whole(lax.optimization_barrier(jnp.sum(rounded(up_parts), axis=0)))
        sigmoid = jax.nn.sigmoid(gate_sum)
        silu_gate = gate_sum * sigmoid
        hidden = (silu_gate * up_sum).astype(jnp.bfloat16)
        hidden_parts = by_hidden(hidden)
        out_parts = over_devices(down_forward, model_in, hidden_parts, down_blocks, down_ids)
        outputs.append(model_whole(lax.optimization_barrier(jnp.sum(rounded(out_parts), axis=1))).astype(jnp.bfloat16))
        back_parts = over_devices(down_backward, model_grad, placeholder, down_blocks, down_ids)
        hidden_grad = hidden_whole(lax.optimization_barrier(jnp.sum(rounded(back_parts), axis=0)))
        gate_act_grad = (hidden_grad * up_sum * sigmoid * (1.0 + gate_sum * (1.0 - sigmoid))).astype(jnp.bfloat16)
        up_act_grad = (hidden_grad * silu_gate).astype(jnp.bfloat16)
        gate_hidden = by_hidden(gate_act_grad)
        up_hidden = by_hidden(up_act_grad)
        in_parts = over_devices(gate_backward, model_in, gate_hidden, gate_blocks, gate_ids)
        in_parts = in_parts + over_devices(gate_backward, model_in, up_hidden, up_blocks, up_ids)
        input_grads.append(model_whole(lax.optimization_barrier(jnp.sum(rounded(in_parts), axis=1))).astype(jnp.bfloat16))
        gate_total = gate_total + rounded(over_devices(gate_weight_grad, model_in, gate_hidden, gate_blocks, gate_ids))
        up_total = up_total + rounded(over_devices(gate_weight_grad, model_in, up_hidden, up_blocks, up_ids))
        down_total = down_total + rounded(over_devices(down_weight_grad, model_grad, hidden_parts, down_blocks, down_ids))
    output = ungroup(jnp.stack(outputs))
    input_grad = ungroup(jnp.stack(input_grads))
    return (output, input_grad, gate_total.astype(jnp.bfloat16), up_total.astype(jnp.bfloat16), down_total.astype(jnp.bfloat16))
```

```python
import functools

import jax
import jax.numpy as jnp
from jax import lax
from jax.experimental import pallas as pl
from jax.experimental.pallas import tpu as pltpu
from jax.sharding import PartitionSpec as P

FF = 14336
SLOTS_PER_STEP = 32
VMEM_LIMIT = 56 << 20


def divisor_up_to(count, limit):
    return max(step for step in range(1, limit + 1) if count % step == 0)


def row_of(slot_id, row_count, col_count):
    factor = -(-(1 << 16) // col_count)
    assert all((i * factor) >> 16 == i // col_count for i in range(row_count * col_count + 1))
    return (slot_id * factor) >> 16


def resident(shape):
    return pl.BlockSpec(shape, lambda step, *ids: (0,) * len(shape))


def stepped(slots, block):
    return pl.BlockSpec((1, 1, slots, block, block), lambda step, *ids: (0, 0, step, 0, 0))


def place(row_count, col_count, ids_ref, step, slots, slot):
    slot_id = ids_ref[step * slots + slot]
    row = row_of(slot_id, row_count, col_count)
    return row, slot_id - row * col_count


def to_hidden_kernel(count, pieces, row_count, col_count, slots, transposed, *refs):
    ids = refs[:count]
    parts = refs[count : count + pieces]
    blocks = refs[count + pieces : 2 * count + pieces]
    sums_out = refs[2 * count + pieces : 3 * count + pieces]
    rows_out = refs[3 * count + pieces]
    source = refs[3 * count + pieces + 1]
    sums = refs[3 * count + pieces + 2 :]
    step = pl.program_id(0)
    block = source.shape[-1]

    @pl.when(step == 0)
    def _():
        for row in range(row_count):
            columns = slice(row * block, (row + 1) * block)
            source[row] = jnp.concatenate([part[:, columns] for part in parts], axis=0)
        source[row_count] = jnp.zeros(source.shape[1:], source.dtype)
        rows_out[...] = source[:row_count]
        for total in sums:
            total[...] = jnp.zeros(total.shape, total.dtype)

    for slot in range(slots):
        for ids_ref, blocks_ref, total in zip(ids, blocks, sums):
            row, col = place(row_count, col_count, ids_ref, step, slots, slot)
            total[col] += lax.dot_general(
                source[row],
                blocks_ref[0, 0, slot],
                (((1,), (1 if transposed else 0,)), ((), ())),
                preferred_element_type=jnp.float32,
            )

    @pl.when(step == pl.num_programs(0) - 1)
    def _():
        for out, total in zip(sums_out, sums):
            out[...] = total[...].astype(out.dtype)


def to_hidden(parts, blocks, ids, row_count, col_count, transposed):
    count, pieces = len(ids), len(parts)
    slot_count, block = blocks[0].shape[2], blocks[0].shape[-1]
    slots = divisor_up_to(slot_count, SLOTS_PER_STEP)
    tokens = sum(part.shape[0] for part in parts)
    sums = jax.ShapeDtypeStruct((col_count, tokens, block), jnp.bfloat16)
    rows = jax.ShapeDtypeStruct((row_count, tokens, block), jnp.bfloat16)
    return pl.pallas_call(
        functools.partial(to_hidden_kernel, count, pieces, row_count, col_count, slots, transposed),
        out_shape=[sums] * count + [rows],
        grid_spec=pltpu.PrefetchScalarGridSpec(
            num_scalar_prefetch=count,
            grid=(slot_count // slots,),
            in_specs=[resident(part.shape) for part in parts] + [stepped(slots, block)] * count,
            out_specs=[resident(sums.shape)] * count + [resident(rows.shape)],
            scratch_shapes=[pltpu.VMEM((row_count + 1, tokens, block), jnp.bfloat16)]
            + [pltpu.VMEM(sums.shape, jnp.float32)] * count,
        ),
        compiler_params=pltpu.CompilerParams(
            dimension_semantics=("arbitrary",), vmem_limit_bytes=VMEM_LIMIT
        ),
        cost_estimate=pl.CostEstimate(
            flops=2 * count * slot_count * tokens * block * block,
            bytes_accessed=2 * count * slot_count * block * block,
            transcendentals=0,
        ),
    )(*ids, *parts, *blocks)


def to_model_kernel(count, pieces, row_count, col_count, slots, transposed, *refs):
    ids = refs[:count]
    sources = refs[count : 2 * count]
    blocks = refs[2 * count : 3 * count]
    outs = refs[3 * count : 3 * count + pieces]
    total = refs[3 * count + pieces]
    step = pl.program_id(0)
    block = total.shape[-1]

    @pl.when(step == 0)
    def _():
        total[...] = jnp.zeros(total.shape, total.dtype)

    for slot in range(slots):
        for ids_ref, source, blocks_ref in zip(ids, sources, blocks):
            row, col = place(row_count, col_count, ids_ref, step, slots, slot)
            total[row] += lax.dot_general(
                source[col],
                blocks_ref[0, 0, slot],
                (((1,), (1 if transposed else 0,)), ((), ())),
                preferred_element_type=jnp.float32,
            )

    @pl.when(step == pl.num_programs(0) - 1)
    def _():
        for piece, out in enumerate(outs):
            height = out.shape[0]
            for row in range(row_count):
                out[:, row * block : (row + 1) * block] = total[
                    row, piece * height : (piece + 1) * height
                ].astype(out.dtype)


def to_model(sources, blocks, ids, row_count, col_count, pieces, transposed):
    count = len(ids)
    slot_count, block = blocks[0].shape[2], blocks[0].shape[-1]
    slots = divisor_up_to(slot_count, SLOTS_PER_STEP)
    tokens = sources[0].shape[1]
    out = jax.ShapeDtypeStruct((tokens // pieces, row_count * block), jnp.bfloat16)
    return pl.pallas_call(
        functools.partial(to_model_kernel, count, pieces, row_count, col_count, slots, transposed),
        out_shape=[out] * pieces,
        grid_spec=pltpu.PrefetchScalarGridSpec(
            num_scalar_prefetch=count,
            grid=(slot_count // slots,),
            in_specs=[resident(source.shape) for source in sources]
            + [stepped(slots, block)] * count,
            out_specs=[resident(out.shape)] * pieces,
            scratch_shapes=[pltpu.VMEM((row_count + 1, tokens, block), jnp.float32)],
        ),
        compiler_params=pltpu.CompilerParams(
            dimension_semantics=("arbitrary",), vmem_limit_bytes=VMEM_LIMIT
        ),
        cost_estimate=pl.CostEstimate(
            flops=2 * count * slot_count * tokens * block * block,
            bytes_accessed=2 * count * slot_count * block * block,
            transcendentals=0,
        ),
    )(*ids, *sources, *blocks)


def block_grads_kernel(count, groups, row_count, col_count, slots, left_is_model, *refs):
    ids = refs[:count]
    model_parts = refs[count : count + groups]
    hidden_parts = [
        refs[count + groups * (1 + i) : count + groups * (2 + i)] for i in range(count)
    ]
    base = count + groups * (1 + count)
    outs = refs[base : base + count]
    model = refs[base + count]
    hiddens = refs[base + count + 1 :]
    step = pl.program_id(0)

    def gather(parts, index, transpose):
        stacked = jnp.concatenate([part[index] for part in parts], axis=0)
        return stacked.T if transpose else stacked

    @pl.when(step == 0)
    def _():
        for row in range(row_count):
            model[row] = gather(model_parts, row, left_is_model)
        model[row_count] = jnp.zeros(model.shape[1:], model.dtype)
        for hidden, parts in zip(hiddens, hidden_parts):
            for col in range(col_count):
                hidden[col] = gather(parts, col, not left_is_model)

    for slot in range(slots):
        for ids_ref, hidden, out in zip(ids, hiddens, outs):
            row, col = place(row_count, col_count, ids_ref, step, slots, slot)
            left, right = (model[row], hidden[col]) if left_is_model else (hidden[col], model[row])
            out[0, 0, slot] = jnp.dot(left, right, preferred_element_type=jnp.float32).astype(
                out.dtype
            )


def block_grads(model_parts, hidden_parts, ids, slot_count, left_is_model):
    count, groups = len(ids), len(model_parts)
    row_count, tokens, block = model_parts[0].shape
    col_count = hidden_parts[0][0].shape[0]
    slots = divisor_up_to(slot_count, SLOTS_PER_STEP)
    total = tokens * groups
    out = jax.ShapeDtypeStruct((1, 1, slot_count, block, block), jnp.bfloat16)

    def held(blocks_held, transposed):
        shape = (block, total) if transposed else (total, block)
        return pltpu.VMEM((blocks_held,) + shape, jnp.bfloat16)

    flat = list(model_parts) + [part for parts in hidden_parts for part in parts]
    return pl.pallas_call(
        functools.partial(
            block_grads_kernel, count, groups, row_count, col_count, slots, left_is_model
        ),
        out_shape=[out] * count,
        grid_spec=pltpu.PrefetchScalarGridSpec(
            num_scalar_prefetch=count,
            grid=(slot_count // slots,),
            in_specs=[resident(part.shape) for part in flat],
            out_specs=[stepped(slots, block)] * count,
            scratch_shapes=[held(row_count + 1, left_is_model)]
            + [held(col_count, not left_is_model)] * count,
        ),
        compiler_params=pltpu.CompilerParams(
            dimension_semantics=("arbitrary",), vmem_limit_bytes=VMEM_LIMIT
        ),
        cost_estimate=pl.CostEstimate(
            flops=2 * count * slot_count * total * block * block,
            bytes_accessed=2 * count * slot_count * block * block,
            transcendentals=0,
        ),
    )(*ids, *flat)


def sent(value, axis, target):
    size = lax.axis_size(axis)
    return lax.ppermute(value, axis, [(i, target(i, size)) for i in range(size)])


def gathered(value, axis):
    size = lax.axis_size(axis)
    return [value] + [
        sent(value, axis, lambda i, n, d=d: (i + d) % n) for d in range(1, size)
    ]


def gathered_by_halves(value, axis):
    size = lax.axis_size(axis)
    if size & (size - 1):
        return gathered(value, axis)
    pieces = [value]
    distance = size // 2
    while distance:
        pieces += [sent(piece, axis, lambda i, n, d=distance: i ^ d) for piece in pieces]
        distance //= 2
    return pieces


def scattered_sum(pieces, axis):
    total = pieces[0].astype(jnp.float32)
    for d in range(1, len(pieces)):
        total += sent(pieces[d], axis, lambda i, n, d=d: (i - d) % n).astype(jnp.float32)
    return total.astype(jnp.bfloat16)


def summed(value, axis):
    size = lax.axis_size(axis)
    return sum(piece.astype(jnp.float32) for piece in gathered(value, axis))


def on_device(tokens, out_grad, gate_blocks, up_blocks, down_blocks, gate_ids, up_ids, down_ids):
    slot_count, block = gate_blocks.shape[2], gate_blocks.shape[-1]
    tile = lax.axis_size("tile")
    row_count = tokens.shape[1] // block
    col_count = FF // tile // block
    grid = (row_count, col_count)
    gate_ids, up_ids, down_ids = (ids.reshape(slot_count) for ids in (gate_ids, up_ids, down_ids))

    token_parts = gathered(tokens, "tile")
    grad_parts = gathered(out_grad, "tile")
    gate_part, up_part, token_rows = to_hidden(
        token_parts, [gate_blocks, up_blocks], [gate_ids, up_ids], *grid, False
    )
    back_part, grad_rows = to_hidden(grad_parts, [down_blocks], [down_ids], *grid, True)
    gate_sum = summed(gate_part, "dp")
    up_sum = summed(up_part, "dp")
    sigmoid = jax.nn.sigmoid(gate_sum)
    silu_gate = gate_sum * sigmoid
    hidden = (silu_gate * up_sum).astype(jnp.bfloat16)
    output = to_model([hidden], [down_blocks], [down_ids], *grid, tile, False)
    hidden_grad = summed(back_part, "dp")
    gate_act_grad = (hidden_grad * up_sum * sigmoid * (1.0 + gate_sum * (1.0 - sigmoid))).astype(
        jnp.bfloat16
    )
    up_act_grad = (hidden_grad * silu_gate).astype(jnp.bfloat16)
    input_grad = to_model(
        [gate_act_grad, up_act_grad],
        [gate_blocks, up_blocks],
        [gate_ids, up_ids],
        *grid,
        tile,
        True,
    )
    all_tokens = gathered_by_halves(token_rows, "replica")
    all_grads = gathered_by_halves(grad_rows, "replica")
    all_hidden = gathered_by_halves(hidden, "replica")
    all_gate = gathered_by_halves(gate_act_grad, "replica")
    all_up = gathered_by_halves(up_act_grad, "replica")
    (down_grad,) = block_grads(all_grads, [all_hidden], [down_ids], slot_count, False)
    gate_grad, up_grad = block_grads(
        all_tokens, [all_gate, all_up], [gate_ids, up_ids], slot_count, True
    )
    return (
        scattered_sum(output, "tile"),
        scattered_sum(input_grad, "tile"),
        gate_grad,
        up_grad,
        down_grad,
    )


def solution(mesh):
    rows = P(("tile", "replica"), "dp")
    blocks = P("dp", "tile", None, None, None)
    ids = P("dp", "tile", None)
    return jax.shard_map(
        on_device,
        mesh=mesh,
        in_specs=(rows, rows, blocks, blocks, blocks, ids, ids, ids),
        out_specs=(rows, rows, blocks, blocks, blocks),
        check_vma=False,
    )
```

```python
import functools

import jax
import jax.numpy as jnp
from jax import lax
from jax.experimental import pallas as pl
from jax.experimental.pallas import tpu as pltpu
from jax.sharding import PartitionSpec as P

FF = 14336
SLOTS_PER_STEP = 32
MIB = 1 << 20


def divisor_up_to(count, limit):
    return max(step for step in range(1, limit + 1) if count % step == 0)


def place(slot_id, row_count, col_count):
    factor = -(-(1 << 16) // col_count)
    assert all((i * factor) >> 16 == i // col_count for i in range(row_count * col_count + 1))
    row = (slot_id * factor) >> 16
    return row, slot_id - row * col_count


def streams(blocks, held, sems):
    slots = held[0].shape[0] // sems.shape[1]

    def copies(step):
        chunk = pl.ds(step * slots, slots)
        return [
            pltpu.make_async_copy(source.at[0, 0, chunk], target.at[chunk], sems.at[i, step])
            for i, (source, target) in enumerate(zip(blocks, held))
        ]

    return copies


def start_all(copies, steps):
    @pl.loop(0, steps)
    def _(step):
        for copy in copies(step):
            copy.start()


def over_slots(slot_count, steps, copies, body):
    slots = slot_count // steps

    @pl.loop(0, steps)
    def _(step):
        for copy in copies(step):
            copy.wait()
        for slot in range(slots):
            body(step * slots + slot)


def stream_scratch(blocks, count):
    slot_count, block = blocks.shape[2], blocks.shape[-1]
    steps = slot_count // divisor_up_to(slot_count, SLOTS_PER_STEP)
    return [pltpu.VMEM((slot_count, block, block), blocks.dtype)] * count + [
        pltpu.SemaphoreType.DMA((count, steps))
    ]


def call(kernel, out_shape, args, smem, scratch, vmem_mib, flops, out_hbm=False):
    memory = [
        pltpu.SMEM if i < smem else pl.ANY if a.ndim == 5 else pltpu.VMEM
        for i, a in enumerate(args)
    ]
    size = sum(a.size * a.dtype.itemsize for a in jax.tree.leaves(out_shape))
    return pl.pallas_call(
        kernel,
        out_shape=out_shape,
        in_specs=[pl.BlockSpec(memory_space=space) for space in memory],
        out_specs=jax.tree.map(
            lambda _: pl.BlockSpec(memory_space=pl.ANY if out_hbm else pltpu.VMEM), out_shape
        ),
        scratch_shapes=scratch,
        compiler_params=pltpu.CompilerParams(vmem_limit_bytes=vmem_mib * MIB),
        cost_estimate=pl.CostEstimate(
            flops=flops,
            bytes_accessed=size + sum(a.size * a.dtype.itemsize for a in args),
            transcendentals=0,
        ),
    )(*args)


def product(left, right):
    return jnp.dot(left, right, preferred_element_type=jnp.float32)


def zero(ref):
    ref[...] = jnp.zeros(ref.shape, ref.dtype)


def gate_up_kernel(grid, gate_ids, up_ids, *refs):
    row_count, col_count = grid
    parts = refs[:-10]
    gate, up, out, rows, source, gate_sum, up_sum, gate_held, up_held, sems = refs[-10:]
    copies = streams((gate, up), (gate_held, up_held), sems)
    start_all(copies, sems.shape[1])
    height = parts[0].shape[0] // 2
    for row in range(row_count):
        columns = slice(row * 128, (row + 1) * 128)
        source[row] = jnp.concatenate([part[:height, columns] for part in parts], axis=0)
        rows[row] = source[row]
        rows[row_count + row] = jnp.concatenate([part[height:, columns] for part in parts], axis=0)
    zero(source.at[row_count])
    zero(gate_sum)
    zero(up_sum)

    def body(slot):
        for ids, held, total in ((gate_ids, gate_held, gate_sum), (up_ids, up_held, up_sum)):
            row, col = place(ids[0, 0, slot], *grid)
            total[col] += product(source[row], held[slot])

    over_slots(gate.shape[2], sems.shape[1], copies, body)
    out[0] = gate_sum[...].astype(out.dtype)
    out[1] = up_sum[...].astype(out.dtype)


def back_kernel(grid, ids, rows, down, out, source, total, held, sems):
    row_count, col_count = grid
    copies = streams((down,), (held,), sems)
    start_all(copies, sems.shape[1])
    for row in range(row_count):
        source[row] = rows[row_count + row].T
    zero(source.at[row_count])
    zero(total)

    def body(slot):
        row, col = place(ids[0, 0, slot], *grid)
        total[col] += product(held[slot], source[row])

    over_slots(down.shape[2], sems.shape[1], copies, body)
    for col in range(col_count):
        out[col] = total[col].T.astype(out.dtype)


def gate_and_up(parts, col):
    return [sum(part[which, col].astype(jnp.float32) for part in parts) for which in (0, 1)]


def down_kernel(grid, ids, *refs):
    row_count, col_count = grid
    parts = refs[:-6]
    down, out, hidden, total, held, sems = refs[-6:]
    copies = streams((down,), (held,), sems)
    start_all(copies, sems.shape[1])
    for col in range(col_count):
        gate_sum, up_sum = gate_and_up(parts, col)
        hidden[col] = (gate_sum * jax.nn.sigmoid(gate_sum) * up_sum).astype(hidden.dtype)
    zero(total)

    def body(slot):
        row, col = place(ids[0, 0, slot], *grid)
        total[row] += product(hidden[col], held[slot])

    over_slots(down.shape[2], sems.shape[1], copies, body)
    for row in range(row_count):
        out[:, row * 128 : (row + 1) * 128] = total[row].astype(out.dtype)


def hidden_kernel(col_count, *refs):
    half = len(refs) // 2
    parts, backs, out = refs[:half], refs[half:-1], refs[-1]
    for col in range(col_count):
        gate_sum, up_sum = gate_and_up(parts, col)
        grad = sum(back[col].astype(jnp.float32) for back in backs)
        sigmoid = jax.nn.sigmoid(gate_sum)
        silu_gate = gate_sum * sigmoid
        out[col] = (silu_gate * up_sum).astype(out.dtype)
        out[col_count + col] = (
            grad * up_sum * sigmoid * (1.0 + gate_sum * (1.0 - sigmoid))
        ).astype(out.dtype)
        out[2 * col_count + col] = (grad * silu_gate).astype(out.dtype)


def input_kernel(grid, gate_ids, up_ids, acts, gate, up, partial, *refs):
    row_count, col_count = grid
    *outs, gate_act, up_act, total, gate_held, up_held, sems = refs
    copies = streams((gate, up), (gate_held, up_held), sems)
    start_all(copies, sems.shape[1])
    for col in range(col_count):
        gate_act[col] = acts[col_count + col].T
        up_act[col] = acts[2 * col_count + col].T
    zero(total)

    def body(slot):
        for ids, held, act in ((gate_ids, gate_held, gate_act), (up_ids, up_held, up_act)):
            row, col = place(ids[0, 0, slot], *grid)
            total[row] += product(held[slot], act[col])

    over_slots(gate.shape[2], sems.shape[1], copies, body)
    height = outs[0].shape[0] // 2
    for piece, out in enumerate(outs):
        out[:height] = partial[piece * height : (piece + 1) * height]
    for row in range(row_count):
        turned = total[row].T.astype(partial.dtype)
        for piece, out in enumerate(outs):
            out[height:, row * 128 : (row + 1) * 128] = turned[piece * height : (piece + 1) * height]


def grads_kernel(grid, groups, gate_ids, up_ids, down_ids, *refs):
    row_count, col_count = grid
    rows, acts = refs[:groups], refs[groups : 2 * groups]
    gate_out, up_out, down_out = refs[2 * groups : 2 * groups + 3]
    x, g, hidden, gate_act, up_act, gate_buf, up_buf, down_buf, sems = refs[2 * groups + 3 :]

    def joined(parts, index):
        return jnp.concatenate([part[index] for part in parts], axis=0)

    for row in range(row_count):
        x[row] = joined(rows, row).T
        g[row] = joined(rows, row_count + row)
    zero(x.at[row_count])
    zero(g.at[row_count])
    for col in range(col_count):
        hidden[col] = joined(acts, col).T
        gate_act[col] = joined(acts, col_count + col)
        up_act[col] = joined(acts, 2 * col_count + col)
    slot_count = gate_buf.shape[0]
    slots = divisor_up_to(slot_count, SLOTS_PER_STEP)
    pairs = ((gate_buf, gate_out), (up_buf, up_out), (down_buf, down_out))

    def copies(step):
        chunk = pl.ds(step * slots, slots)
        return [
            pltpu.make_async_copy(buf.at[chunk], out.at[0, 0, chunk], sems.at[i, step])
            for i, (buf, out) in enumerate(pairs)
        ]

    @pl.loop(0, slot_count // slots)
    def _(step):
        for index in range(slots):
            slot = step * slots + index
            for ids, act, buf in ((gate_ids, gate_act, gate_buf), (up_ids, up_act, up_buf)):
                row, col = place(ids[0, 0, slot], *grid)
                buf[slot] = product(x[row], act[col]).astype(buf.dtype)
            row, col = place(down_ids[0, 0, slot], *grid)
            down_buf[slot] = product(hidden[col], g[row]).astype(down_buf.dtype)
        for copy in copies(step):
            copy.start()

    @pl.loop(0, slot_count // slots)
    def _(step):
        for copy in copies(step):
            copy.wait()


def sent(value, axis, target):
    size = lax.axis_size(axis)
    return lax.ppermute(value, axis, [(i, target(i, size)) for i in range(size)])


def gathered(value, axis):
    size = lax.axis_size(axis)
    return [value] + [
        sent(value, axis, lambda i, n, d=d: (i + d) % n) for d in range(1, size)
    ]


def doublings(axis):
    size = lax.axis_size(axis)
    if size & (size - 1):
        return [lambda pieces: gathered(pieces[0], axis)]
    return [
        lambda pieces, d=1 << bit: pieces
        + [sent(piece, axis, lambda i, n: i ^ d) for piece in pieces]
        for bit in reversed(range(size.bit_length() - 1))
    ]


def scattered(pieces, axis):
    return [pieces[0]] + [
        sent(pieces[d], axis, lambda i, n, d=d: (i - d) % n) for d in range(1, len(pieces))
    ]


def on_device(tokens, out_grad, gate_blocks, up_blocks, down_blocks, gate_ids, up_ids, down_ids):
    slot_count, block = gate_blocks.shape[2], gate_blocks.shape[-1]
    tile, groups = lax.axis_size("tile"), lax.axis_size("replica")
    height = tokens.shape[0]
    group = height * tile
    row_count = tokens.shape[1] // block
    col_count = FF // tile // block
    grid = (row_count, col_count)
    bf16, f32 = jnp.bfloat16, jnp.float32
    shape = jax.ShapeDtypeStruct
    step_flops = 2 * slot_count * group * block * block

    parts = gathered(jnp.concatenate([tokens, out_grad], axis=0), "tile")
    gate_up, rows = call(
        functools.partial(gate_up_kernel, grid),
        [shape((2, col_count, group, block), bf16), shape((2 * row_count, group, block), bf16)],
        [gate_ids, up_ids, *parts, gate_blocks, up_blocks],
        2,
        [pltpu.VMEM((row_count + 1, group, block), bf16)]
        + [pltpu.VMEM((col_count, group, block), f32)] * 2
        + stream_scratch(gate_blocks, 2),
        48,
        2 * step_flops,
    )
    back = call(
        functools.partial(back_kernel, grid),
        shape((col_count, group, block), bf16),
        [down_ids, rows, down_blocks],
        1,
        [
            pltpu.VMEM((row_count + 1, block, group), bf16),
            pltpu.VMEM((col_count, block, group), f32),
            *stream_scratch(down_blocks, 1),
        ],
        48,
        step_flops,
    )
    first_doubling, *later_doublings = doublings("replica")
    all_rows = first_doubling([rows])
    gate_up_parts = gathered(gate_up, "dp")
    gate_up_parts, all_rows = lax.optimization_barrier((gate_up_parts, all_rows))
    for doubling in later_doublings:
        all_rows = doubling(all_rows)
    partial = call(
        functools.partial(down_kernel, grid),
        shape((group, row_count * block), bf16),
        [down_ids, *gate_up_parts, down_blocks],
        1,
        [
            pltpu.VMEM((col_count, group, block), bf16),
            pltpu.VMEM((row_count + 1, group, block), f32),
            *stream_scratch(down_blocks, 1),
        ],
        48,
        step_flops,
    )
    back_parts, partial, all_rows = lax.optimization_barrier(
        (gathered(back, "dp"), partial, all_rows)
    )
    acts = call(
        functools.partial(hidden_kernel, col_count),
        shape((3 * col_count, group, block), bf16),
        [*gate_up_parts, *back_parts],
        0,
        [],
        8,
        1,
    )
    all_acts = first_doubling([acts])
    pieces = call(
        functools.partial(input_kernel, grid),
        [shape((2 * height, row_count * block), bf16)] * tile,
        [gate_ids, up_ids, acts, gate_blocks, up_blocks, partial],
        2,
        [pltpu.VMEM((col_count, block, group), bf16)] * 2
        + [pltpu.VMEM((row_count + 1, block, group), f32)]
        + stream_scratch(gate_blocks, 2),
        48,
        2 * step_flops,
    )
    pieces, all_acts[1:] = lax.optimization_barrier((pieces, all_acts[1:]))
    for doubling in later_doublings:
        all_acts = doubling(all_acts)
    total = group * groups
    slots = divisor_up_to(slot_count, SLOTS_PER_STEP)
    grads = call(
        functools.partial(grads_kernel, grid, groups),
        [shape(gate_blocks.shape, bf16)] * 3,
        [gate_ids, up_ids, down_ids, *all_rows, *all_acts],
        3,
        [
            pltpu.VMEM((row_count + 1, block, total), bf16),
            pltpu.VMEM((row_count + 1, total, block), bf16),
            pltpu.VMEM((col_count, block, total), bf16),
            pltpu.VMEM((col_count, total, block), bf16),
            pltpu.VMEM((col_count, total, block), bf16),
        ]
        + [pltpu.VMEM((slot_count, block, block), bf16)] * 3
        + [pltpu.SemaphoreType.DMA((3, slot_count // slots))],
        44,
        3 * step_flops * groups,
        out_hbm=True,
    )
    pieces, grads = lax.optimization_barrier((scattered(pieces, "tile"), grads))
    summed = sum(piece.astype(f32) for piece in pieces).astype(bf16)
    return (summed[:height], summed[height:], *grads)


def solution(mesh):
    rows = P(("tile", "replica"), "dp")
    blocks = P("dp", "tile", None, None, None)
    ids = P("dp", "tile", None)
    return jax.shard_map(
        on_device,
        mesh=mesh,
        in_specs=(rows, rows, blocks, blocks, blocks, ids, ids, ids),
        out_specs=(rows, rows, blocks, blocks, blocks),
        check_vma=False,
    )
```

```python
import functools

import jax
import jax.numpy as jnp
from jax import lax
from jax.experimental import pallas as pl
from jax.experimental.pallas import tpu as pltpu
from jax.sharding import PartitionSpec as P

FF = 14336
SLOTS_PER_STEP = 32
MIB = 1 << 20


def divisor_up_to(count, limit):
    return max(step for step in range(1, limit + 1) if count % step == 0)


def place(slot_id, row_count, col_count):
    factor = -(-(1 << 16) // col_count)
    assert all((i * factor) >> 16 == i // col_count for i in range(row_count * col_count + 1))
    row = (slot_id * factor) >> 16
    return row, slot_id - row * col_count


def streams(blocks, held, sems):
    slots = held[0].shape[0] // sems.shape[1]

    def copies(step):
        chunk = pl.ds(step * slots, slots)
        return [
            pltpu.make_async_copy(source.at[0, 0, chunk], target.at[chunk], sems.at[i, step])
            for i, (source, target) in enumerate(zip(blocks, held))
        ]

    return copies


def start_all(copies, steps):
    @pl.loop(0, steps)
    def _(step):
        for copy in copies(step):
            copy.start()


def over_slots(slot_count, steps, copies, body):
    slots = slot_count // steps

    @pl.loop(0, steps)
    def _(step):
        for copy in copies(step):
            copy.wait()
        for slot in range(slots):
            body(step * slots + slot)


def stream_scratch(blocks, count):
    slot_count, block = blocks.shape[2], blocks.shape[-1]
    steps = slot_count // divisor_up_to(slot_count, SLOTS_PER_STEP)
    return [pltpu.VMEM((slot_count, block, block), blocks.dtype)] * count + [
        pltpu.SemaphoreType.DMA((count, steps))
    ]


def call(kernel, out_shape, args, smem, scratch, vmem_mib, flops, out_hbm=False):
    memory = [
        pltpu.SMEM if i < smem else pl.ANY if a.ndim == 5 else pltpu.VMEM
        for i, a in enumerate(args)
    ]
    size = sum(a.size * a.dtype.itemsize for a in jax.tree.leaves(out_shape))
    return pl.pallas_call(
        kernel,
        out_shape=out_shape,
        in_specs=[pl.BlockSpec(memory_space=space) for space in memory],
        out_specs=jax.tree.map(
            lambda _: pl.BlockSpec(memory_space=pl.ANY if out_hbm else pltpu.VMEM), out_shape
        ),
        scratch_shapes=scratch,
        compiler_params=pltpu.CompilerParams(vmem_limit_bytes=vmem_mib * MIB),
        cost_estimate=pl.CostEstimate(
            flops=20 * flops,
            bytes_accessed=size + sum(a.size * a.dtype.itemsize for a in args),
            transcendentals=0,
        ),
    )(*args)


def product(left, right):
    return jnp.dot(left, right, preferred_element_type=jnp.float32)


def zero(ref):
    ref[...] = jnp.zeros(ref.shape, ref.dtype)


def block_of(parts, row):
    return jnp.concatenate([part[:, row * 128 : (row + 1) * 128] for part in parts], axis=0)


def gate_up_kernel(grid, gate_ids, up_ids, *refs):
    row_count, col_count = grid
    parts = refs[:-10]
    gate, up, out, rows, source, gate_sum, up_sum, gate_held, up_held, sems = refs[-10:]
    copies = streams((gate, up), (gate_held, up_held), sems)
    start_all(copies, sems.shape[1])
    for row in range(row_count):
        source[row] = block_of(parts, row)
        rows[row] = source[row]
    zero(source.at[row_count])
    zero(gate_sum)
    zero(up_sum)

    def body(slot):
        for ids, held, total in ((gate_ids, gate_held, gate_sum), (up_ids, up_held, up_sum)):
            row, col = place(ids[0, 0, slot], *grid)
            total[col] += product(source[row], held[slot])

    over_slots(gate.shape[2], sems.shape[1], copies, body)
    out[0] = gate_sum[...].astype(out.dtype)
    out[1] = up_sum[...].astype(out.dtype)


def back_kernel(grid, ids, token_rows, *refs):
    row_count, col_count = grid
    parts = refs[:-7]
    down, out, rows, source, total, held, sems = refs[-7:]
    copies = streams((down,), (held,), sems)
    start_all(copies, sems.shape[1])
    rows[:row_count] = token_rows[...]
    for row in range(row_count):
        block = block_of(parts, row)
        rows[row_count + row] = block
        source[row] = block.T
    zero(source.at[row_count])
    zero(total)

    def body(slot):
        row, col = place(ids[0, 0, slot], *grid)
        total[col] += product(held[slot], source[row])

    over_slots(down.shape[2], sems.shape[1], copies, body)
    for col in range(col_count):
        out[col] = total[col].T.astype(out.dtype)


def gate_and_up(parts, col):
    return [sum(part[which, col].astype(jnp.float32) for part in parts) for which in (0, 1)]


def down_kernel(grid, ids, *refs):
    row_count, col_count = grid
    parts = refs[:-6]
    down, out, hidden, total, held, sems = refs[-6:]
    copies = streams((down,), (held,), sems)
    start_all(copies, sems.shape[1])
    for col in range(col_count):
        gate_sum, up_sum = gate_and_up(parts, col)
        hidden[col] = (gate_sum * jax.nn.sigmoid(gate_sum) * up_sum).astype(hidden.dtype)
    zero(total)

    def body(slot):
        row, col = place(ids[0, 0, slot], *grid)
        total[row] += product(hidden[col], held[slot])

    over_slots(down.shape[2], sems.shape[1], copies, body)
    for row in range(row_count):
        out[:, row * 128 : (row + 1) * 128] = total[row].astype(out.dtype)


def hidden_kernel(col_count, *refs):
    half = len(refs) // 2
    parts, backs, out = refs[:half], refs[half:-1], refs[-1]
    for col in range(col_count):
        gate_sum, up_sum = gate_and_up(parts, col)
        grad = sum(back[col].astype(jnp.float32) for back in backs)
        sigmoid = jax.nn.sigmoid(gate_sum)
        silu_gate = gate_sum * sigmoid
        out[col] = (silu_gate * up_sum).astype(out.dtype)
        out[col_count + col] = (
            grad * up_sum * sigmoid * (1.0 + gate_sum * (1.0 - sigmoid))
        ).astype(out.dtype)
        out[2 * col_count + col] = (grad * silu_gate).astype(out.dtype)


def input_kernel(grid, gate_ids, up_ids, acts, gate, up, partial, *refs):
    row_count, col_count = grid
    *outs, gate_act, up_act, total, gate_held, up_held, sems = refs
    copies = streams((gate, up), (gate_held, up_held), sems)
    start_all(copies, sems.shape[1])
    for col in range(col_count):
        gate_act[col] = acts[col_count + col].T
        up_act[col] = acts[2 * col_count + col].T
    zero(total)

    def body(slot):
        for ids, held, act in ((gate_ids, gate_held, gate_act), (up_ids, up_held, up_act)):
            row, col = place(ids[0, 0, slot], *grid)
            total[row] += product(held[slot], act[col])

    over_slots(gate.shape[2], sems.shape[1], copies, body)
    height = outs[0].shape[0] // 2
    for piece, out in enumerate(outs):
        out[:height] = partial[piece * height : (piece + 1) * height]
    for row in range(row_count):
        turned = total[row].T.astype(partial.dtype)
        for piece, out in enumerate(outs):
            out[height:, row * 128 : (row + 1) * 128] = turned[piece * height : (piece + 1) * height]


def grads_kernel(grid, groups, gate_ids, up_ids, down_ids, *refs):
    row_count, col_count = grid
    rows, acts = refs[:groups], refs[groups : 2 * groups]
    gate_out, up_out, down_out = refs[2 * groups : 2 * groups + 3]
    x, g, hidden, gate_act, up_act, gate_buf, up_buf, down_buf, sems = refs[2 * groups + 3 :]

    def joined(parts, index):
        return jnp.concatenate([part[index] for part in parts], axis=0)

    for row in range(row_count):
        x[row] = joined(rows, row).T
        g[row] = joined(rows, row_count + row)
    zero(x.at[row_count])
    zero(g.at[row_count])
    for col in range(col_count):
        hidden[col] = joined(acts, col).T
        gate_act[col] = joined(acts, col_count + col)
        up_act[col] = joined(acts, 2 * col_count + col)
    slot_count = gate_buf.shape[0]
    slots = divisor_up_to(slot_count, SLOTS_PER_STEP)
    pairs = ((gate_buf, gate_out), (up_buf, up_out), (down_buf, down_out))

    def copies(step):
        chunk = pl.ds(step * slots, slots)
        return [
            pltpu.make_async_copy(buf.at[chunk], out.at[0, 0, chunk], sems.at[i, step])
            for i, (buf, out) in enumerate(pairs)
        ]

    @pl.loop(0, slot_count // slots)
    def _(step):
        for index in range(slots):
            slot = step * slots + index
            for ids, act, buf in ((gate_ids, gate_act, gate_buf), (up_ids, up_act, up_buf)):
                row, col = place(ids[0, 0, slot], *grid)
                buf[slot] = product(x[row], act[col]).astype(buf.dtype)
            row, col = place(down_ids[0, 0, slot], *grid)
            down_buf[slot] = product(hidden[col], g[row]).astype(down_buf.dtype)
        for copy in copies(step):
            copy.start()

    @pl.loop(0, slot_count // slots)
    def _(step):
        for copy in copies(step):
            copy.wait()


def sent(value, axis, target):
    size = lax.axis_size(axis)
    return lax.ppermute(value, axis, [(i, target(i, size)) for i in range(size)])


def gathered(value, axis):
    size = lax.axis_size(axis)
    return [value] + [
        sent(value, axis, lambda i, n, d=d: (i + d) % n) for d in range(1, size)
    ]


def doublings(axis):
    size = lax.axis_size(axis)
    if size & (size - 1):
        return [lambda pieces: gathered(pieces[0], axis)]
    return [
        lambda pieces, d=1 << bit: pieces
        + [sent(piece, axis, lambda i, n: i ^ d) for piece in pieces]
        for bit in reversed(range(size.bit_length() - 1))
    ]


def scattered(pieces, axis):
    return [pieces[0]] + [
        sent(pieces[d], axis, lambda i, n, d=d: (i - d) % n) for d in range(1, len(pieces))
    ]


def on_device(tokens, out_grad, gate_blocks, up_blocks, down_blocks, gate_ids, up_ids, down_ids):
    slot_count, block = gate_blocks.shape[2], gate_blocks.shape[-1]
    tile, groups = lax.axis_size("tile"), lax.axis_size("replica")
    height = tokens.shape[0]
    group = height * tile
    row_count = tokens.shape[1] // block
    col_count = FF // tile // block
    grid = (row_count, col_count)
    bf16, f32 = jnp.bfloat16, jnp.float32
    shape = jax.ShapeDtypeStruct
    step_flops = 2 * slot_count * group * block * block

    token_parts, grad_parts = gathered(tokens, "tile"), gathered(out_grad, "tile")
    gate_up, token_rows = call(
        functools.partial(gate_up_kernel, grid),
        [shape((2, col_count, group, block), bf16), shape((row_count, group, block), bf16)],
        [gate_ids, up_ids, *token_parts, gate_blocks, up_blocks],
        2,
        [pltpu.VMEM((row_count + 1, group, block), bf16)]
        + [pltpu.VMEM((col_count, group, block), f32)] * 2
        + stream_scratch(gate_blocks, 2),
        48,
        2 * step_flops,
    )
    back, rows = call(
        functools.partial(back_kernel, grid),
        [shape((col_count, group, block), bf16), shape((2 * row_count, group, block), bf16)],
        [down_ids, token_rows, *grad_parts, down_blocks],
        1,
        [
            pltpu.VMEM((row_count + 1, block, group), bf16),
            pltpu.VMEM((col_count, block, group), f32),
            *stream_scratch(down_blocks, 1),
        ],
        48,
        step_flops,
    )
    first_doubling, *later_doublings = doublings("replica")
    all_rows = first_doubling([rows])
    gate_up_parts = gathered(gate_up, "dp")
    gate_up_parts, back = lax.optimization_barrier((gate_up_parts, back))
    partial = call(
        functools.partial(down_kernel, grid),
        shape((group, row_count * block), bf16),
        [down_ids, *gate_up_parts, down_blocks],
        1,
        [
            pltpu.VMEM((col_count, group, block), bf16),
            pltpu.VMEM((row_count + 1, group, block), f32),
            *stream_scratch(down_blocks, 1),
        ],
        48,
        step_flops,
    )
    back_parts, partial, all_rows = lax.optimization_barrier(
        (gathered(back, "dp"), partial, all_rows)
    )
    acts = call(
        functools.partial(hidden_kernel, col_count),
        shape((3 * col_count, group, block), bf16),
        [*gate_up_parts, *back_parts],
        0,
        [],
        8,
        1,
    )
    all_acts = first_doubling([acts])
    for doubling in later_doublings:
        all_rows = doubling(all_rows)
    partial, all_rows = lax.optimization_barrier((partial, all_rows))
    pieces = call(
        functools.partial(input_kernel, grid),
        [shape((2 * height, row_count * block), bf16)] * tile,
        [gate_ids, up_ids, acts, gate_blocks, up_blocks, partial],
        2,
        [pltpu.VMEM((col_count, block, group), bf16)] * 2
        + [pltpu.VMEM((row_count + 1, block, group), f32)]
        + stream_scratch(gate_blocks, 2),
        48,
        2 * step_flops,
    )
    pieces, all_acts[1:] = lax.optimization_barrier((pieces, all_acts[1:]))
    for doubling in later_doublings:
        all_acts = doubling(all_acts)
    total = group * groups
    slots = divisor_up_to(slot_count, SLOTS_PER_STEP)
    grads = call(
        functools.partial(grads_kernel, grid, groups),
        [shape(gate_blocks.shape, bf16)] * 3,
        [gate_ids, up_ids, down_ids, *all_rows, *all_acts],
        3,
        [
            pltpu.VMEM((row_count + 1, block, total), bf16),
            pltpu.VMEM((row_count + 1, total, block), bf16),
            pltpu.VMEM((col_count, block, total), bf16),
            pltpu.VMEM((col_count, total, block), bf16),
            pltpu.VMEM((col_count, total, block), bf16),
        ]
        + [pltpu.VMEM((slot_count, block, block), bf16)] * 3
        + [pltpu.SemaphoreType.DMA((3, slot_count // slots))],
        44,
        3 * step_flops * groups,
        out_hbm=True,
    )
    pieces, grads = lax.optimization_barrier((scattered(pieces, "tile"), grads))
    summed = sum(piece.astype(f32) for piece in pieces).astype(bf16)
    return (summed[:height], summed[height:], *grads)


def solution(mesh):
    rows = P(("tile", "replica"), "dp")
    blocks = P("dp", "tile", None, None, None)
    ids = P("dp", "tile", None)
    return jax.shard_map(
        on_device,
        mesh=mesh,
        in_specs=(rows, rows, blocks, blocks, blocks, ids, ids, ids),
        out_specs=(rows, rows, blocks, blocks, blocks),
        check_vma=False,
    )
```

```python
import functools

import jax
import jax.numpy as jnp
from jax import lax
from jax.experimental import pallas as pl
from jax.experimental.pallas import tpu as pltpu
from jax.sharding import PartitionSpec as P

FF = 14336
SLOTS_PER_STEP = 32
MIB = 1 << 20


def divisor_up_to(count, limit):
    return max(step for step in range(1, limit + 1) if count % step == 0)


def place(slot_id, row_count, col_count):
    factor = -(-(1 << 16) // col_count)
    assert all((i * factor) >> 16 == i // col_count for i in range(row_count * col_count + 1))
    row = (slot_id * factor) >> 16
    return row, slot_id - row * col_count


def turned_scratch(blocks, count):
    slots = divisor_up_to(blocks.shape[2] // 2, SLOTS_PER_STEP)
    return [pltpu.VMEM((slots,) + blocks.shape[3:], blocks.dtype)] * (2 * count)


def streams(blocks, held, sems):
    slots = held[0].shape[0] // sems.shape[1]

    def copies(step):
        chunk = pl.ds(step * slots, slots)
        return [
            pltpu.make_async_copy(source.at[0, 0, chunk], target.at[chunk], sems.at[i, step])
            for i, (source, target) in enumerate(zip(blocks, held))
        ]

    return copies


def start_all(copies, steps):
    @pl.loop(0, steps)
    def _(step):
        for copy in copies(step):
            copy.start()


def over_slots(slot_count, steps, copies, body):
    slots = slot_count // steps

    @pl.loop(0, steps)
    def _(step):
        for copy in copies(step):
            copy.wait()
        for slot in range(slots):
            body(step * slots + slot)


def over_turned_slots(held, turned, steps, copies, body):
    assert steps % 2 == 0
    slots = held[0].shape[0] // steps

    def turn(step, slot, half):
        for source, targets in zip(held, turned):
            targets[half][slot] = source[step * slots + slot].T

    for copy in copies(0):
        copy.wait()
    for slot in range(slots):
        turn(0, slot, 0)

    @pl.loop(0, steps // 2)
    def _(pair):
        for half in range(2):
            step = 2 * pair + half
            later = jnp.minimum(step + 1, steps - 1)

            @pl.when(step + 1 < steps)
            def _():
                for copy in copies(later):
                    copy.wait()

            for slot in range(slots):
                body(step * slots + slot, [targets[half].at[slot] for targets in turned])
                turn(later, slot, 1 - half)


def stream_scratch(blocks, count, halves=1):
    slot_count, block = blocks.shape[2], blocks.shape[-1]
    steps = halves * (slot_count // halves // divisor_up_to(slot_count // halves, SLOTS_PER_STEP))
    return [pltpu.VMEM((slot_count, block, block), blocks.dtype)] * count + [
        pltpu.SemaphoreType.DMA((count, steps))
    ]


def in_hbm(value):
    return pltpu.with_memory_space_constraint(value, pltpu.HBM)


def call(kernel, out_shape, args, smem, scratch, vmem_mib, flops, out_hbm=False, fetched=0):
    ahead = smem + fetched
    memory = [
        pl.ANY if i < ahead or a.ndim == 5 else pltpu.VMEM for i, a in enumerate(args)
    ]
    args = [in_hbm(a) if i < ahead else a for i, a in enumerate(args)]
    inner = kernel

    def kernel(*refs):
        held, sems = refs[-1 - ahead : -1], refs[-1]
        copies = [
            pltpu.make_async_copy(ids, target, sems.at[i])
            for i, (ids, target) in enumerate(zip(refs[:ahead], held))
        ]
        for copy in copies:
            copy.start()

        def arrive():
            for copy in copies:
                copy.wait()

        inner(arrive, *held, *refs[ahead : -1 - ahead])

    if ahead:
        scratch = scratch + [pltpu.SMEM(a.shape, a.dtype) for a in args[:smem]]
        scratch += [pltpu.VMEM(a.shape, a.dtype) for a in args[smem:ahead]]
        scratch += [pltpu.SemaphoreType.DMA((ahead,))]
    else:
        kernel = inner
    size = sum(a.size * a.dtype.itemsize for a in jax.tree.leaves(out_shape))
    return pl.pallas_call(
        kernel,
        out_shape=out_shape,
        in_specs=[pl.BlockSpec(memory_space=space) for space in memory],
        out_specs=jax.tree.map(
            lambda _: pl.BlockSpec(memory_space=pl.ANY if out_hbm else pltpu.VMEM), out_shape
        ),
        scratch_shapes=scratch,
        compiler_params=pltpu.CompilerParams(vmem_limit_bytes=vmem_mib * MIB),
        cost_estimate=pl.CostEstimate(
            flops=20 * flops,
            bytes_accessed=size + sum(a.size * a.dtype.itemsize for a in args),
            transcendentals=0,
        ),
    )(*args)


def product(left, right):
    return jnp.dot(left, right, preferred_element_type=jnp.float32)


def zero(ref):
    ref[...] = jnp.zeros(ref.shape, ref.dtype)


def block_of(parts, row):
    return jnp.concatenate([part[:, row * 128 : (row + 1) * 128] for part in parts], axis=0)


def gate_up_kernel(grid, arrive, gate_ids, up_ids, *refs):
    row_count, col_count = grid
    parts = refs[:-10]
    gate, up, out, rows, source, gate_sum, up_sum, gate_held, up_held, sems = refs[-10:]
    copies = streams((gate, up), (gate_held, up_held), sems)
    start_all(copies, sems.shape[1])
    zero(source.at[row_count])
    zero(gate_sum)
    zero(up_sum)
    arrive()
    for row in range(row_count):
        source[row] = block_of(parts, row)
        rows[row] = source[row]

    def body(slot):
        for ids, held, total in ((gate_ids, gate_held, gate_sum), (up_ids, up_held, up_sum)):
            row, col = place(ids[0, 0, slot], *grid)
            total[col] += product(source[row], held[slot])

    over_slots(gate.shape[2], sems.shape[1], copies, body)
    out[0] = gate_sum[...].astype(out.dtype)
    out[1] = up_sum[...].astype(out.dtype)


def back_kernel(grid, arrive, ids, token_rows, *refs):
    row_count, col_count = grid
    parts = refs[:-9]
    down, out, rows, source, total, near, far, held, sems = refs[-9:]
    copies = streams((down,), (held,), sems)
    start_all(copies, sems.shape[1])
    rows[:row_count] = token_rows[...]
    for row in range(row_count):
        source[row] = block_of(parts, row)
        rows[row_count + row] = source[row]
    zero(source.at[row_count])
    zero(total)

    def body(slot, turned):
        row, col = place(ids[0, 0, slot], *grid)
        total[col] += product(source[row], turned[0][...])

    arrive()
    over_turned_slots((held,), ((near, far),), sems.shape[1], copies, body)
    out[...] = total[...].astype(out.dtype)


def run_back(grid, down_ids, token_rows, grad_parts, down_blocks, flops):
    (row_count, col_count), block = grid, down_blocks.shape[-1]
    group = token_rows.shape[1]
    shape = jax.ShapeDtypeStruct
    return call(
        functools.partial(back_kernel, grid),
        [
            shape((col_count, group, block), jnp.bfloat16),
            shape((2 * row_count, group, block), jnp.bfloat16),
        ],
        [down_ids, token_rows, *grad_parts, down_blocks],
        1,
        [
            pltpu.VMEM((row_count + 1, group, block), jnp.bfloat16),
            pltpu.VMEM((col_count, group, block), jnp.float32),
            *turned_scratch(down_blocks, 1),
            *stream_scratch(down_blocks, 1, 2),
        ],
        48,
        flops,
    )


def gate_and_up(parts, col):
    return [sum(part[which, col].astype(jnp.float32) for part in parts) for which in (0, 1)]


def down_kernel(grid, arrive, ids, *refs):
    row_count, col_count = grid
    parts = refs[:-6]
    down, out, hidden, total, held, sems = refs[-6:]
    copies = streams((down,), (held,), sems)
    start_all(copies, sems.shape[1])
    for col in range(col_count):
        gate_sum, up_sum = gate_and_up(parts, col)
        hidden[col] = (gate_sum * jax.nn.sigmoid(gate_sum) * up_sum).astype(hidden.dtype)
    zero(total)

    def body(slot):
        row, col = place(ids[0, 0, slot], *grid)
        total[row] += product(hidden[col], held[slot])

    arrive()
    over_slots(down.shape[2], sems.shape[1], copies, body)
    for row in range(row_count):
        out[:, row * 128 : (row + 1) * 128] = total[row].astype(out.dtype)


def hidden_kernel(col_count, *refs):
    half = len(refs) // 2
    parts, backs, out = refs[:half], refs[half:-1], refs[-1]
    for col in range(col_count):
        gate_sum, up_sum = gate_and_up(parts, col)
        grad = sum(back[col].astype(jnp.float32) for back in backs)
        sigmoid = jax.nn.sigmoid(gate_sum)
        silu_gate = gate_sum * sigmoid
        out[col] = (silu_gate * up_sum).astype(out.dtype)
        out[col_count + col] = (
            grad * up_sum * sigmoid * (1.0 + gate_sum * (1.0 - sigmoid))
        ).astype(out.dtype)
        out[2 * col_count + col] = (grad * silu_gate).astype(out.dtype)


def input_kernel(grid, arrive, gate_ids, up_ids, acts, gate, up, partial, *refs):
    row_count, col_count = grid
    *outs, total, gate_near, gate_far, up_near, up_far, gate_held, up_held, sems = refs
    copies = streams((gate, up), (gate_held, up_held), sems)
    start_all(copies, sems.shape[1])
    zero(total)

    def body(slot, turned):
        for ids, blocks, which in ((gate_ids, turned[0], 1), (up_ids, turned[1], 2)):
            row, col = place(ids[0, 0, slot], *grid)
            total[row] += product(acts[which * col_count + col], blocks[...])

    halves = ((gate_near, gate_far), (up_near, up_far))
    arrive()
    over_turned_slots((gate_held, up_held), halves, sems.shape[1], copies, body)
    height = outs[0].shape[0] // 2
    for piece, out in enumerate(outs):
        tokens = slice(piece * height, (piece + 1) * height)
        out[:height] = partial[tokens]
        for row in range(row_count):
            out[height:, row * 128 : (row + 1) * 128] = total[row, tokens].astype(out.dtype)


def run_input(grid, gate_ids, up_ids, acts, gate_blocks, up_blocks, partial, tile, flops):
    (row_count, _), block = grid, gate_blocks.shape[-1]
    group = partial.shape[0]
    return call(
        functools.partial(input_kernel, grid),
        [jax.ShapeDtypeStruct((2 * group // tile, row_count * block), jnp.bfloat16)] * tile,
        [gate_ids, up_ids, acts, gate_blocks, up_blocks, partial],
        2,
        [
            pltpu.VMEM((row_count + 1, group, block), jnp.float32),
            *turned_scratch(gate_blocks, 2),
            *stream_scratch(gate_blocks, 2, 2),
        ],
        48,
        flops,
    )


def grads_kernel(grid, groups, arrive, gate_ids, up_ids, down_ids, *refs):
    row_count, col_count = grid
    rows, acts = refs[:groups], refs[groups : 2 * groups]
    gate_out, up_out, down_out = refs[2 * groups : 2 * groups + 3]
    x, g, hidden, gate_act, up_act, gate_buf, up_buf, down_buf, sems = refs[2 * groups + 3 :]

    def joined(parts, index):
        return jnp.concatenate([part[index] for part in parts], axis=0)

    for row in range(row_count):
        x[row] = joined(rows, row).T
        g[row] = joined(rows, row_count + row)
    zero(x.at[row_count])
    zero(g.at[row_count])
    for col in range(col_count):
        hidden[col] = joined(acts, col).T
        gate_act[col] = joined(acts, col_count + col)
        up_act[col] = joined(acts, 2 * col_count + col)
    slot_count = gate_buf.shape[0]
    slots = divisor_up_to(slot_count, SLOTS_PER_STEP)
    pairs = ((gate_buf, gate_out), (up_buf, up_out), (down_buf, down_out))

    def copies(step):
        chunk = pl.ds(step * slots, slots)
        return [
            pltpu.make_async_copy(buf.at[chunk], out.at[0, 0, chunk], sems.at[i, step])
            for i, (buf, out) in enumerate(pairs)
        ]

    arrive()

    @pl.loop(0, slot_count // slots)
    def _(step):
        for index in range(slots):
            slot = step * slots + index
            for ids, act, buf in ((gate_ids, gate_act, gate_buf), (up_ids, up_act, up_buf)):
                row, col = place(ids[0, 0, slot], *grid)
                buf[slot] = product(x[row], act[col]).astype(buf.dtype)
            row, col = place(down_ids[0, 0, slot], *grid)
            down_buf[slot] = product(hidden[col], g[row]).astype(down_buf.dtype)
        for copy in copies(step):
            copy.start()

    @pl.loop(0, slot_count // slots)
    def _(step):
        for copy in copies(step):
            copy.wait()


def sent(value, axis, target):
    size = lax.axis_size(axis)
    return lax.ppermute(value, axis, [(i, target(i, size)) for i in range(size)])


def beyond(device, distance, size):
    return (device + distance) % size if size & (size - 1) else device ^ distance


def gathered(value, axis):
    size = lax.axis_size(axis)
    return [value] + [
        sent(value, axis, lambda i, n, d=d: beyond(i, d, n)) for d in range(1, size)
    ]


def doublings(axis):
    size = lax.axis_size(axis)
    if size & (size - 1):
        return [lambda pieces: gathered(pieces[0], axis)]
    return [
        lambda pieces, d=1 << bit: pieces
        + [sent(piece, axis, lambda i, n: i ^ d) for piece in pieces]
        for bit in reversed(range(size.bit_length() - 1))
    ]


def scattered(pieces, axis):
    size = lax.axis_size(axis)
    sign = -1 if size & (size - 1) else 1
    return [pieces[0]] + [
        sent(pieces[d], axis, lambda i, n, d=d: beyond(i, sign * d, n)) for d in range(1, size)
    ]


def on_device(tokens, out_grad, gate_blocks, up_blocks, down_blocks, gate_ids, up_ids, down_ids):
    slot_count, block = gate_blocks.shape[2], gate_blocks.shape[-1]
    tile, groups = lax.axis_size("tile"), lax.axis_size("replica")
    height = tokens.shape[0]
    group = height * tile
    row_count = tokens.shape[1] // block
    col_count = FF // tile // block
    grid = (row_count, col_count)
    bf16, f32 = jnp.bfloat16, jnp.float32
    shape = jax.ShapeDtypeStruct
    step_flops = 2 * slot_count * group * block * block

    token_parts, grad_parts = gathered(tokens, "tile"), gathered(out_grad, "tile")
    gate_up, token_rows = call(
        functools.partial(gate_up_kernel, grid),
        [shape((2, col_count, group, block), bf16), shape((row_count, group, block), bf16)],
        [gate_ids, up_ids, *token_parts, gate_blocks, up_blocks],
        2,
        [pltpu.VMEM((row_count + 1, group, block), bf16)]
        + [pltpu.VMEM((col_count, group, block), f32)] * 2
        + stream_scratch(gate_blocks, 2),
        48,
        2 * step_flops,
        fetched=1,
    )
    back, rows = run_back(grid, down_ids, token_rows, grad_parts, down_blocks, step_flops)
    first_doubling, *later_doublings = doublings("replica")
    all_rows = first_doubling([rows])
    gate_up_parts = gathered(gate_up, "dp")
    gate_up_parts, back = lax.optimization_barrier((gate_up_parts, back))
    partial = call(
        functools.partial(down_kernel, grid),
        shape((group, row_count * block), bf16),
        [down_ids, *gate_up_parts, down_blocks],
        1,
        [
            pltpu.VMEM((col_count, group, block), bf16),
            pltpu.VMEM((row_count + 1, group, block), f32),
            *stream_scratch(down_blocks, 1),
        ],
        48,
        step_flops,
    )
    back_parts, partial = lax.optimization_barrier((gathered(back, "dp"), partial))
    acts = call(
        functools.partial(hidden_kernel, col_count),
        shape((3 * col_count, group, block), bf16),
        [*gate_up_parts, *back_parts],
        0,
        [],
        8,
        1,
    )
    all_acts = first_doubling([acts])
    partial, all_rows[1:] = lax.optimization_barrier((partial, all_rows[1:]))
    for doubling in later_doublings:
        all_rows = doubling(all_rows)
    pieces = run_input(
        grid, gate_ids, up_ids, acts, gate_blocks, up_blocks, partial, tile, 2 * step_flops
    )
    _, all_acts[1:] = lax.optimization_barrier((pieces, all_acts[1:]))
    for doubling in later_doublings:
        all_acts = doubling(all_acts)
    total = group * groups
    slots = divisor_up_to(slot_count, SLOTS_PER_STEP)
    grads = call(
        functools.partial(grads_kernel, grid, groups),
        [shape(gate_blocks.shape, bf16)] * 3,
        [gate_ids, up_ids, down_ids, *all_rows, *all_acts],
        3,
        [
            pltpu.VMEM((row_count + 1, block, total), bf16),
            pltpu.VMEM((row_count + 1, total, block), bf16),
            pltpu.VMEM((col_count, block, total), bf16),
            pltpu.VMEM((col_count, total, block), bf16),
            pltpu.VMEM((col_count, total, block), bf16),
        ]
        + [pltpu.VMEM((slot_count, block, block), bf16)] * 3
        + [pltpu.SemaphoreType.DMA((3, slot_count // slots))],
        44,
        3 * step_flops * groups,
        out_hbm=True,
    )
    pieces, grads = lax.optimization_barrier((scattered(pieces, "tile"), grads))
    summed = sum(piece.astype(f32) for piece in pieces).astype(bf16)
    return (summed[:height], summed[height:], *grads)


def solution(mesh):
    rows = P(("tile", "replica"), "dp")
    blocks = P("dp", "tile", None, None, None)
    ids = P("dp", "tile", None)
    return jax.shard_map(
        on_device,
        mesh=mesh,
        in_specs=(rows, rows, blocks, blocks, blocks, ids, ids, ids),
        out_specs=(rows, rows, blocks, blocks, blocks),
        check_vma=False,
    )
```

```python
import functools

import jax
import jax.numpy as jnp
from jax import lax
from jax.experimental import pallas as pl
from jax.experimental.pallas import tpu as pltpu
from jax.sharding import PartitionSpec as P

FF = 14336
SLOTS_PER_STEP = 32
MIB = 1 << 20


def divisor_up_to(count, limit):
    return max(step for step in range(1, limit + 1) if count % step == 0)


def place(slot_id, row_count, col_count):
    factor = -(-(1 << 16) // col_count)
    assert all((i * factor) >> 16 == i // col_count for i in range(row_count * col_count + 1))
    row = (slot_id * factor) >> 16
    return row, slot_id - row * col_count


def turned_scratch(blocks, count):
    slots = divisor_up_to(blocks.shape[2] // 2, SLOTS_PER_STEP)
    return [pltpu.VMEM((slots,) + blocks.shape[3:], blocks.dtype)] * (2 * count)


def streams(blocks, held, sems):
    slots = held[0].shape[0] // sems.shape[1]

    def copies(step):
        chunk = pl.ds(step * slots, slots)
        return [
            pltpu.make_async_copy(source.at[0, 0, chunk], target.at[chunk], sems.at[i, step])
            for i, (source, target) in enumerate(zip(blocks, held))
        ]

    return copies


def start_all(copies, steps):
    @pl.loop(0, steps)
    def _(step):
        for copy in copies(step):
            copy.start()


def over_slots(slot_count, steps, copies, body):
    slots = slot_count // steps

    @pl.loop(0, steps)
    def _(step):
        for copy in copies(step):
            copy.wait()
        for slot in range(slots):
            body(step * slots + slot)


def over_turned_slots(held, turned, steps, copies, body):
    assert steps % 2 == 0
    slots = held[0].shape[0] // steps

    def turn(step, slot, half):
        for source, targets in zip(held, turned):
            targets[half][slot] = source[step * slots + slot].T

    for copy in copies(0):
        copy.wait()
    for slot in range(slots):
        turn(0, slot, 0)

    @pl.loop(0, steps // 2)
    def _(pair):
        for half in range(2):
            step = 2 * pair + half
            later = jnp.minimum(step + 1, steps - 1)

            @pl.when(step + 1 < steps)
            def _():
                for copy in copies(later):
                    copy.wait()

            for slot in range(slots):
                body(step * slots + slot, [targets[half].at[slot] for targets in turned])
                turn(later, slot, 1 - half)


def stream_scratch(blocks, count, halves=1):
    slot_count, block = blocks.shape[2], blocks.shape[-1]
    steps = halves * (slot_count // halves // divisor_up_to(slot_count // halves, SLOTS_PER_STEP))
    return [pltpu.VMEM((slot_count, block, block), blocks.dtype)] * count + [
        pltpu.SemaphoreType.DMA((count, steps))
    ]


def in_hbm(value):
    return pltpu.with_memory_space_constraint(value, pltpu.HBM)


def call(kernel, out_shape, args, smem, scratch, vmem_mib, flops, out_hbm=False, fetched=0):
    ahead = smem + fetched
    memory = [
        pl.ANY if i < ahead or a.ndim == 5 else pltpu.VMEM for i, a in enumerate(args)
    ]
    args = [in_hbm(a) if i < ahead else a for i, a in enumerate(args)]
    inner = kernel

    def kernel(*refs):
        held, sems = refs[-1 - ahead : -1], refs[-1]
        copies = [
            pltpu.make_async_copy(ids, target, sems.at[i])
            for i, (ids, target) in enumerate(zip(refs[:ahead], held))
        ]
        for copy in copies:
            copy.start()

        def arrive():
            for copy in copies:
                copy.wait()

        inner(arrive, *held, *refs[ahead : -1 - ahead])

    if ahead:
        scratch = scratch + [pltpu.SMEM(a.shape, a.dtype) for a in args[:smem]]
        scratch += [pltpu.VMEM(a.shape, a.dtype) for a in args[smem:ahead]]
        scratch += [pltpu.SemaphoreType.DMA((ahead,))]
    else:
        kernel = inner
    size = sum(a.size * a.dtype.itemsize for a in jax.tree.leaves(out_shape))
    return pl.pallas_call(
        kernel,
        out_shape=out_shape,
        in_specs=[pl.BlockSpec(memory_space=space) for space in memory],
        out_specs=jax.tree.map(
            lambda _: pl.BlockSpec(memory_space=pl.ANY if out_hbm else pltpu.VMEM), out_shape
        ),
        scratch_shapes=scratch,
        compiler_params=pltpu.CompilerParams(vmem_limit_bytes=vmem_mib * MIB),
        cost_estimate=pl.CostEstimate(
            flops=20 * flops,
            bytes_accessed=size + sum(a.size * a.dtype.itemsize for a in args),
            transcendentals=0,
        ),
    )(*args)


def product(left, right):
    return jnp.dot(left, right, preferred_element_type=jnp.float32)


def zero(ref):
    ref[...] = jnp.zeros(ref.shape, ref.dtype)


def block_of(parts, row):
    return jnp.concatenate([part[:, row * 128 : (row + 1) * 128] for part in parts], axis=0)


def gate_up_kernel(grid, arrive, gate_ids, up_ids, *refs):
    row_count, col_count = grid
    parts = refs[:-9]
    gate, up, out, source, gate_sum, up_sum, gate_held, up_held, sems = refs[-9:]
    copies = streams((gate, up), (gate_held, up_held), sems)
    start_all(copies, sems.shape[1])
    zero(source.at[row_count])
    zero(gate_sum)
    zero(up_sum)
    arrive()
    for row in range(row_count):
        source[row] = block_of(parts, row)

    def body(slot):
        for ids, held, total in ((gate_ids, gate_held, gate_sum), (up_ids, up_held, up_sum)):
            row, col = place(ids[0, 0, slot], *grid)
            total[col] += product(source[row], held[slot])

    over_slots(gate.shape[2], sems.shape[1], copies, body)
    out[0] = gate_sum[...].astype(out.dtype)
    out[1] = up_sum[...].astype(out.dtype)


def rows_kernel(row_count, *refs):
    *parts, out = refs
    half = len(parts) // 2
    for row in range(row_count):
        out[row] = block_of(parts[:half], row)
        out[row_count + row] = block_of(parts[half:], row)
    zero(out.at[2 * row_count])


def back_kernel(grid, arrive, ids, rows, down, out, total, near, far, held, sems):
    row_count, col_count = grid
    copies = streams((down,), (held,), sems)
    start_all(copies, sems.shape[1])
    zero(total)
    arrive()

    def body(slot, turned):
        row, col = place(ids[0, 0, slot], *grid)
        total[col] += product(rows[row_count + row], turned[0][...])

    over_turned_slots((held,), ((near, far),), sems.shape[1], copies, body)
    out[...] = total[...].astype(out.dtype)


def gate_and_up(parts, col):
    return [sum(part[which, col].astype(jnp.float32) for part in parts) for which in (0, 1)]


def hidden_kernel(col_count, *refs):
    half = len(refs) // 2
    parts, backs, out = refs[:half], refs[half:-1], refs[-1]
    for col in range(col_count):
        gate_sum, up_sum = gate_and_up(parts, col)
        grad = sum(back[col].astype(jnp.float32) for back in backs)
        sigmoid = jax.nn.sigmoid(gate_sum)
        silu_gate = gate_sum * sigmoid
        out[col] = (silu_gate * up_sum).astype(out.dtype)
        out[col_count + col] = (
            grad * up_sum * sigmoid * (1.0 + gate_sum * (1.0 - sigmoid))
        ).astype(out.dtype)
        out[2 * col_count + col] = (grad * silu_gate).astype(out.dtype)


def model_kernel(grid, arrive, gate_ids, up_ids, down_ids, acts, gate, up, down, *refs):
    row_count, col_count = grid
    *outs, y_sum, x_sum, gate_near, gate_far, up_near, up_far = refs[:-4]
    gate_held, up_held, down_held, sems = refs[-4:]
    copies = streams((gate, up, down), (gate_held, up_held, down_held), sems)
    start_all(copies, sems.shape[1])
    zero(y_sum)
    zero(x_sum)
    arrive()

    def body(slot, turned):
        for ids, blocks, which in ((gate_ids, turned[0], 1), (up_ids, turned[1], 2)):
            row, col = place(ids[0, 0, slot], *grid)
            x_sum[row] += product(acts[which * col_count + col], blocks[...])
        row, col = place(down_ids[0, 0, slot], *grid)
        y_sum[row] += product(acts[col], down_held[slot])

    halves = ((gate_near, gate_far), (up_near, up_far))
    over_turned_slots((gate_held, up_held), halves, sems.shape[1], copies, body)
    height = outs[0].shape[0] // 2
    for piece, out in enumerate(outs):
        tokens = slice(piece * height, (piece + 1) * height)
        for row in range(row_count):
            columns = slice(row * 128, (row + 1) * 128)
            out[:height, columns] = y_sum[row, tokens].astype(out.dtype)
            out[height:, columns] = x_sum[row, tokens].astype(out.dtype)


def grads_kernel(grid, groups, arrive, gate_ids, up_ids, down_ids, *refs):
    row_count, col_count = grid
    rows, acts = refs[:groups], refs[groups : 2 * groups]
    gate_out, up_out, down_out = refs[2 * groups : 2 * groups + 3]
    x, g, hidden, gate_act, up_act, gate_buf, up_buf, down_buf, sems = refs[2 * groups + 3 :]

    def joined(parts, index):
        return jnp.concatenate([part[index] for part in parts], axis=0)

    for row in range(row_count):
        x[row] = joined(rows, row).T
        g[row] = joined(rows, row_count + row)
    zero(x.at[row_count])
    zero(g.at[row_count])
    for col in range(col_count):
        hidden[col] = joined(acts, col).T
        gate_act[col] = joined(acts, col_count + col)
        up_act[col] = joined(acts, 2 * col_count + col)
    slot_count = gate_buf.shape[0]
    slots = divisor_up_to(slot_count, SLOTS_PER_STEP)
    pairs = ((gate_buf, gate_out), (up_buf, up_out), (down_buf, down_out))

    def copies(step):
        chunk = pl.ds(step * slots, slots)
        return [
            pltpu.make_async_copy(buf.at[chunk], out.at[0, 0, chunk], sems.at[i, step])
            for i, (buf, out) in enumerate(pairs)
        ]

    arrive()

    @pl.loop(0, slot_count // slots)
    def _(step):
        for index in range(slots):
            slot = step * slots + index
            for ids, act, buf in ((gate_ids, gate_act, gate_buf), (up_ids, up_act, up_buf)):
                row, col = place(ids[0, 0, slot], *grid)
                buf[slot] = product(x[row], act[col]).astype(buf.dtype)
            row, col = place(down_ids[0, 0, slot], *grid)
            down_buf[slot] = product(hidden[col], g[row]).astype(down_buf.dtype)
        for copy in copies(step):
            copy.start()

    @pl.loop(0, slot_count // slots)
    def _(step):
        for copy in copies(step):
            copy.wait()


def sent(value, axis, target):
    size = lax.axis_size(axis)
    return lax.ppermute(value, axis, [(i, target(i, size)) for i in range(size)])


def beyond(device, distance, size):
    return (device + distance) % size if size & (size - 1) else device ^ distance


def gathered(value, axis):
    size = lax.axis_size(axis)
    return [value] + [
        sent(value, axis, lambda i, n, d=d: beyond(i, d, n)) for d in range(1, size)
    ]


def doublings(axis):
    size = lax.axis_size(axis)
    if size & (size - 1):
        return [lambda pieces: gathered(pieces[0], axis)]
    return [
        lambda pieces, d=1 << bit: pieces
        + [sent(piece, axis, lambda i, n: i ^ d) for piece in pieces]
        for bit in reversed(range(size.bit_length() - 1))
    ]


def scattered(pieces, axis):
    size = lax.axis_size(axis)
    sign = -1 if size & (size - 1) else 1
    return [pieces[0]] + [
        sent(pieces[d], axis, lambda i, n, d=d: beyond(i, sign * d, n)) for d in range(1, size)
    ]


def on_device(tokens, out_grad, gate_blocks, up_blocks, down_blocks, gate_ids, up_ids, down_ids):
    slot_count, block = gate_blocks.shape[2], gate_blocks.shape[-1]
    tile, groups = lax.axis_size("tile"), lax.axis_size("replica")
    height = tokens.shape[0]
    group = height * tile
    row_count = tokens.shape[1] // block
    col_count = FF // tile // block
    grid = (row_count, col_count)
    bf16, f32 = jnp.bfloat16, jnp.float32
    shape = jax.ShapeDtypeStruct
    step_flops = 2 * slot_count * group * block * block

    token_parts, grad_parts = gathered(tokens, "tile"), gathered(out_grad, "tile")
    gate_up = call(
        functools.partial(gate_up_kernel, grid),
        shape((2, col_count, group, block), bf16),
        [gate_ids, up_ids, *token_parts, gate_blocks, up_blocks],
        2,
        [pltpu.VMEM((row_count + 1, group, block), bf16)]
        + [pltpu.VMEM((col_count, group, block), f32)] * 2
        + stream_scratch(gate_blocks, 2),
        48,
        2 * step_flops,
        fetched=1,
    )
    _, grad_parts = lax.optimization_barrier((gate_up, grad_parts))
    rows = call(
        functools.partial(rows_kernel, row_count),
        shape((2 * row_count + 1, group, block), bf16),
        [*token_parts, *grad_parts],
        0,
        [],
        8,
        1,
    )
    first_doubling, *later_doublings = doublings("replica")
    all_rows = first_doubling([rows])
    back = call(
        functools.partial(back_kernel, grid),
        shape((col_count, group, block), bf16),
        [down_ids, rows, down_blocks],
        1,
        [
            pltpu.VMEM((col_count, group, block), f32),
            *turned_scratch(down_blocks, 1),
            *stream_scratch(down_blocks, 1, 2),
        ],
        48,
        step_flops,
    )
    gate_up_parts = gathered(gate_up, "dp")
    gate_up_parts, back = lax.optimization_barrier((gate_up_parts, back))
    back_parts, all_rows[1:] = lax.optimization_barrier((gathered(back, "dp"), all_rows[1:]))
    acts = call(
        functools.partial(hidden_kernel, col_count),
        shape((3 * col_count, group, block), bf16),
        [*gate_up_parts, *back_parts],
        0,
        [],
        8,
        1,
    )
    all_acts = first_doubling([acts])
    for doubling in later_doublings:
        all_rows = doubling(all_rows)
    pieces = call(
        functools.partial(model_kernel, grid),
        [shape((2 * height, row_count * block), bf16)] * tile,
        [gate_ids, up_ids, down_ids, acts, gate_blocks, up_blocks, down_blocks],
        3,
        [pltpu.VMEM((row_count + 1, group, block), f32)] * 2
        + [*turned_scratch(gate_blocks, 2), *stream_scratch(gate_blocks, 3, 2)],
        48,
        3 * step_flops,
    )
    _, all_acts[1:] = lax.optimization_barrier((pieces, all_acts[1:]))
    for doubling in later_doublings:
        all_acts = doubling(all_acts)
    total = group * groups
    slots = divisor_up_to(slot_count, SLOTS_PER_STEP)
    grads = call(
        functools.partial(grads_kernel, grid, groups),
        [shape(gate_blocks.shape, bf16)] * 3,
        [gate_ids, up_ids, down_ids, *all_rows, *all_acts],
        3,
        [
            pltpu.VMEM((row_count + 1, block, total), bf16),
            pltpu.VMEM((row_count + 1, total, block), bf16),
            pltpu.VMEM((col_count, block, total), bf16),
            pltpu.VMEM((col_count, total, block), bf16),
            pltpu.VMEM((col_count, total, block), bf16),
        ]
        + [pltpu.VMEM((slot_count, block, block), bf16)] * 3
        + [pltpu.SemaphoreType.DMA((3, slot_count // slots))],
        44,
        3 * step_flops * groups,
        out_hbm=True,
    )
    pieces, grads = lax.optimization_barrier((scattered(pieces, "tile"), grads))
    summed = sum(piece.astype(f32) for piece in pieces).astype(bf16)
    return (summed[:height], summed[height:], *grads)


def solution(mesh):
    rows = P(("tile", "replica"), "dp")
    blocks = P("dp", "tile", None, None, None)
    ids = P("dp", "tile", None)
    return jax.shard_map(
        on_device,
        mesh=mesh,
        in_specs=(rows, rows, blocks, blocks, blocks, ids, ids, ids),
        out_specs=(rows, rows, blocks, blocks, blocks),
        check_vma=False,
    )
```

```python
import functools

import jax
import jax.numpy as jnp
from jax import lax
from jax.experimental import pallas as pl
from jax.experimental.pallas import tpu as pltpu
from jax.sharding import PartitionSpec as P

FF = 14336
SLOTS_PER_STEP = 32
MIB = 1 << 20


def divisor_up_to(count, limit):
    return max(step for step in range(1, limit + 1) if count % step == 0)


def place(slot_id, row_count, col_count):
    factor = -(-(1 << 16) // col_count)
    assert all((i * factor) >> 16 == i // col_count for i in range(row_count * col_count + 1))
    row = (slot_id * factor) >> 16
    return row, slot_id - row * col_count


def turned_scratch(blocks, count):
    slots = divisor_up_to(blocks.shape[2] // 2, SLOTS_PER_STEP)
    return [pltpu.VMEM((slots,) + blocks.shape[3:], blocks.dtype)] * (2 * count)


def streams(blocks, held, sems):
    slots = held[0].shape[0] // sems.shape[1]

    def copies(step):
        chunk = pl.ds(step * slots, slots)
        return [
            pltpu.make_async_copy(source.at[0, 0, chunk], target.at[chunk], sems.at[i, step])
            for i, (source, target) in enumerate(zip(blocks, held))
        ]

    return copies


def start_all(copies, steps):
    @pl.loop(0, steps)
    def _(step):
        for copy in copies(step):
            copy.start()


def over_slots(slot_count, steps, copies, body):
    slots = slot_count // steps

    @pl.loop(0, steps)
    def _(step):
        for copy in copies(step):
            copy.wait()
        for slot in range(slots):
            body(step * slots + slot)


def over_turned_slots(held, turned, steps, copies, body):
    assert steps % 2 == 0
    slots = held[0].shape[0] // steps

    def turn(step, slot, half):
        for source, targets in zip(held, turned):
            targets[half][slot] = source[step * slots + slot].T

    for copy in copies(0):
        copy.wait()
    for slot in range(slots):
        turn(0, slot, 0)

    @pl.loop(0, steps // 2)
    def _(pair):
        for half in range(2):
            step = 2 * pair + half
            later = jnp.minimum(step + 1, steps - 1)

            @pl.when(step + 1 < steps)
            def _():
                for copy in copies(later):
                    copy.wait()

            for slot in range(slots):
                body(step * slots + slot, [targets[half].at[slot] for targets in turned])
                turn(later, slot, 1 - half)


def stream_scratch(blocks, count, halves=1, limit=SLOTS_PER_STEP):
    slot_count, block = blocks.shape[2], blocks.shape[-1]
    steps = halves * (slot_count // halves // divisor_up_to(slot_count // halves, limit))
    return [pltpu.VMEM((slot_count, block, block), blocks.dtype)] * count + [
        pltpu.SemaphoreType.DMA((count, steps))
    ]


def in_hbm(value):
    return pltpu.with_memory_space_constraint(value, pltpu.HBM)


def call(kernel, out_shape, args, smem, scratch, vmem_mib, flops, out_hbm=False, fetched=0):
    ahead = smem + fetched
    memory = [
        pl.ANY if i < ahead or a.ndim == 5 else pltpu.VMEM for i, a in enumerate(args)
    ]
    args = [in_hbm(a) if i < ahead else a for i, a in enumerate(args)]
    inner = kernel

    def kernel(*refs):
        held, sems = refs[-1 - ahead : -1], refs[-1]
        copies = [
            pltpu.make_async_copy(ids, target, sems.at[i])
            for i, (ids, target) in enumerate(zip(refs[:ahead], held))
        ]
        for copy in copies:
            copy.start()

        def arrive():
            for copy in copies:
                copy.wait()

        inner(arrive, *held, *refs[ahead : -1 - ahead])

    if ahead:
        scratch = scratch + [pltpu.SMEM(a.shape, a.dtype) for a in args[:smem]]
        scratch += [pltpu.VMEM(a.shape, a.dtype) for a in args[smem:ahead]]
        scratch += [pltpu.SemaphoreType.DMA((ahead,))]
    else:
        kernel = inner
    size = sum(a.size * a.dtype.itemsize for a in jax.tree.leaves(out_shape))
    return pl.pallas_call(
        kernel,
        out_shape=out_shape,
        in_specs=[pl.BlockSpec(memory_space=space) for space in memory],
        out_specs=jax.tree.map(
            lambda _: pl.BlockSpec(memory_space=pl.ANY if out_hbm else pltpu.VMEM), out_shape
        ),
        scratch_shapes=scratch,
        compiler_params=pltpu.CompilerParams(vmem_limit_bytes=vmem_mib * MIB),
        cost_estimate=pl.CostEstimate(
            flops=20 * flops,
            bytes_accessed=size + sum(a.size * a.dtype.itemsize for a in args),
            transcendentals=0,
        ),
    )(*args)


def product(left, right):
    return jnp.dot(left, right, preferred_element_type=jnp.float32)


def zero(ref):
    ref[...] = jnp.zeros(ref.shape, ref.dtype)


def block_of(parts, row):
    return jnp.concatenate([part[:, row * 128 : (row + 1) * 128] for part in parts], axis=0)


def gate_up_kernel(grid, arrive, gate_ids, up_ids, *refs):
    row_count, col_count = grid
    parts = refs[:-9]
    gate, up, out, source, gate_sum, up_sum, gate_held, up_held, sems = refs[-9:]
    copies = streams((gate, up), (gate_held, up_held), sems)
    start_all(copies, sems.shape[1])
    zero(source.at[row_count])
    zero(gate_sum)
    zero(up_sum)
    arrive()
    for row in range(row_count):
        source[row] = block_of(parts, row)

    def body(slot):
        for ids, held, total in ((gate_ids, gate_held, gate_sum), (up_ids, up_held, up_sum)):
            row, col = place(ids[0, 0, slot], *grid)
            total[col] += product(source[row], held[slot])

    over_slots(gate.shape[2], sems.shape[1], copies, body)
    out[0] = gate_sum[...].astype(out.dtype)
    out[1] = up_sum[...].astype(out.dtype)


def rows_kernel(row_count, *refs):
    *parts, out = refs
    half = len(parts) // 2
    for row in range(row_count):
        out[row] = block_of(parts[:half], row)
        out[row_count + row] = block_of(parts[half:], row)
    zero(out.at[2 * row_count])


def back_kernel(grid, arrive, ids, rows, down, out, total, near, far, held, sems):
    row_count, col_count = grid
    copies = streams((down,), (held,), sems)
    start_all(copies, sems.shape[1])
    zero(total)
    arrive()

    def body(slot, turned):
        row, col = place(ids[0, 0, slot], *grid)
        total[col] += product(rows[row_count + row], turned[0][...])

    over_turned_slots((held,), ((near, far),), sems.shape[1], copies, body)
    out[...] = total[...].astype(out.dtype)


def gate_and_up(parts, col):
    return [sum(part[which, col].astype(jnp.float32) for part in parts) for which in (0, 1)]


def hidden_kernel(col_count, summands, row_arrays, row_blocks, *refs):
    parts, backs = refs[:summands], refs[summands : 2 * summands]
    rows = refs[2 * summands : 2 * summands + row_arrays]
    acts, *packs = refs[2 * summands + row_arrays :]
    for col in range(col_count):
        gate_sum, up_sum = gate_and_up(parts, col)
        grad = sum(back[col].astype(jnp.float32) for back in backs)
        sigmoid = jax.nn.sigmoid(gate_sum)
        silu_gate = gate_sum * sigmoid
        acts[col] = (silu_gate * up_sum).astype(acts.dtype)
        acts[col_count + col] = (
            grad * up_sum * sigmoid * (1.0 + gate_sum * (1.0 - sigmoid))
        ).astype(acts.dtype)
        acts[2 * col_count + col] = (grad * silu_gate).astype(acts.dtype)
    for pack in packs:
        for place_of, held in enumerate(rows):
            pack[place_of * row_blocks : (place_of + 1) * row_blocks] = held[:row_blocks]
        pack[len(rows) * row_blocks :] = acts[...]


def model_kernel(grid, arrive, gate_ids, up_ids, down_ids, acts, gate, up, down, *refs):
    row_count, col_count = grid
    *outs, y_sum, x_sum, gate_near, gate_far, up_near, up_far = refs[:-4]
    gate_held, up_held, down_held, sems = refs[-4:]
    copies = streams((gate, up, down), (gate_held, up_held, down_held), sems)
    start_all(copies, sems.shape[1])
    zero(y_sum)
    zero(x_sum)
    arrive()

    def body(slot, turned):
        for ids, blocks, which in ((gate_ids, turned[0], 1), (up_ids, turned[1], 2)):
            row, col = place(ids[0, 0, slot], *grid)
            x_sum[row] += product(acts[which * col_count + col], blocks[...])
        row, col = place(down_ids[0, 0, slot], *grid)
        y_sum[row] += product(acts[col], down_held[slot])

    halves = ((gate_near, gate_far), (up_near, up_far))
    over_turned_slots((gate_held, up_held), halves, sems.shape[1], copies, body)
    height = outs[0].shape[0] // 2
    for piece, out in enumerate(outs):
        tokens = slice(piece * height, (piece + 1) * height)
        for row in range(row_count):
            columns = slice(row * 128, (row + 1) * 128)
            out[:height, columns] = y_sum[row, tokens].astype(out.dtype)
            out[height:, columns] = x_sum[row, tokens].astype(out.dtype)


def grads_kernel(grid, rows, acts, arrive, gate_ids, up_ids, down_ids, *refs):
    row_count, col_count = grid
    gate_out, up_out, down_out, x, g, hidden, gate_act, up_act = refs[-12:-4]
    gate_buf, up_buf, down_buf, sems = refs[-4:]

    def joined(groups, index):
        return jnp.concatenate([refs[array][first + index] for array, first in groups], axis=0)

    for row in range(row_count):
        x[row] = joined(rows, row).T
        g[row] = joined(rows, row_count + row)
    zero(x.at[row_count])
    zero(g.at[row_count])
    for col in range(col_count):
        hidden[col] = joined(acts, col).T
        gate_act[col] = joined(acts, col_count + col)
        up_act[col] = joined(acts, 2 * col_count + col)
    slot_count = gate_buf.shape[0]
    slots = divisor_up_to(slot_count, SLOTS_PER_STEP)
    pairs = ((gate_buf, gate_out), (up_buf, up_out), (down_buf, down_out))

    def copies(step):
        chunk = pl.ds(step * slots, slots)
        return [
            pltpu.make_async_copy(buf.at[chunk], out.at[0, 0, chunk], sems.at[i, step])
            for i, (buf, out) in enumerate(pairs)
        ]

    arrive()

    @pl.loop(0, slot_count // slots)
    def _(step):
        for index in range(slots):
            slot = step * slots + index
            for ids, act, buf in ((gate_ids, gate_act, gate_buf), (up_ids, up_act, up_buf)):
                row, col = place(ids[0, 0, slot], *grid)
                buf[slot] = product(x[row], act[col]).astype(buf.dtype)
            row, col = place(down_ids[0, 0, slot], *grid)
            down_buf[slot] = product(hidden[col], g[row]).astype(down_buf.dtype)
        for copy in copies(step):
            copy.start()

    @pl.loop(0, slot_count // slots)
    def _(step):
        for copy in copies(step):
            copy.wait()


def sent(value, axis, target):
    size = lax.axis_size(axis)
    return lax.ppermute(value, axis, [(i, target(i, size)) for i in range(size)])


def beyond(device, distance, size):
    return (device + distance) % size if size & (size - 1) else device ^ distance


def gathered(value, axis):
    size = lax.axis_size(axis)
    return [value] + [
        sent(value, axis, lambda i, n, d=d: beyond(i, d, n)) for d in range(1, size)
    ]


def across(value, distance):
    return sent(value, "replica", lambda i, n: i ^ distance)


def scattered(pieces, axis):
    size = lax.axis_size(axis)
    sign = -1 if size & (size - 1) else 1
    return [pieces[0]] + [
        sent(pieces[d], axis, lambda i, n, d=d: beyond(i, sign * d, n)) for d in range(1, size)
    ]


def on_device(tokens, out_grad, gate_blocks, up_blocks, down_blocks, gate_ids, up_ids, down_ids):
    slot_count, block = gate_blocks.shape[2], gate_blocks.shape[-1]
    tile, groups = lax.axis_size("tile"), lax.axis_size("replica")
    height = tokens.shape[0]
    group = height * tile
    row_count = tokens.shape[1] // block
    col_count = FF // tile // block
    grid = (row_count, col_count)
    bf16, f32 = jnp.bfloat16, jnp.float32
    shape = jax.ShapeDtypeStruct
    step_flops = 2 * slot_count * group * block * block

    token_parts, grad_parts = gathered(tokens, "tile"), gathered(out_grad, "tile")
    gate_up = call(
        functools.partial(gate_up_kernel, grid),
        shape((2, col_count, group, block), bf16),
        [gate_ids, up_ids, *token_parts, gate_blocks, up_blocks],
        2,
        [pltpu.VMEM((row_count + 1, group, block), bf16)]
        + [pltpu.VMEM((col_count, group, block), f32)] * 2
        + stream_scratch(gate_blocks, 2, limit=48),
        48,
        2 * step_flops,
        fetched=1,
    )
    _, grad_parts = lax.optimization_barrier((gate_up, grad_parts))
    rows = call(
        functools.partial(rows_kernel, row_count),
        shape((2 * row_count + 1, group, block), bf16),
        [*token_parts, *grad_parts],
        0,
        [],
        8,
        1,
    )
    packed = groups == 4
    far_rows = across(rows, 2) if packed else None
    back = call(
        functools.partial(back_kernel, grid),
        shape((col_count, group, block), bf16),
        [down_ids, rows, down_blocks],
        1,
        [
            pltpu.VMEM((col_count, group, block), f32),
            *turned_scratch(down_blocks, 1),
            *stream_scratch(down_blocks, 1, 2),
        ],
        48,
        step_flops,
    )
    gate_up_parts = gathered(gate_up, "dp")
    gate_up_parts, _ = lax.optimization_barrier((gate_up_parts, back))
    back_parts, far_rows = lax.optimization_barrier((gathered(back, "dp"), far_rows))
    acts_shape = shape((3 * col_count, group, block), bf16)
    row_blocks = 2 * row_count
    pack_shape = shape((2 * row_blocks + 3 * col_count, group, block), bf16)
    acts, *pack = call(
        functools.partial(hidden_kernel, col_count, len(back_parts), 2 * packed, row_blocks),
        [acts_shape, pack_shape] if packed else [acts_shape],
        [*gate_up_parts, *back_parts, *([rows, far_rows] if packed else [])],
        0,
        [],
        8,
        1,
    )
    far_acts = across(acts, 2) if packed else None
    pieces = call(
        functools.partial(model_kernel, grid),
        [shape((2 * height, row_count * block), bf16)] * tile,
        [gate_ids, up_ids, down_ids, acts, gate_blocks, up_blocks, down_blocks],
        3,
        [pltpu.VMEM((row_count + 1, group, block), f32)] * 2
        + [*turned_scratch(gate_blocks, 2), *stream_scratch(gate_blocks, 3, 2)],
        48,
        3 * step_flops,
    )
    if packed:
        _, far_acts = lax.optimization_barrier((pieces, far_acts))
        arrays = [rows, far_rows, across(pack[0], 1), acts, far_acts, across(far_acts, 1)]
        rows_at = ((0, 0), (1, 0), (2, 0), (2, row_blocks))
        acts_at = ((3, 0), (4, 0), (2, 2 * row_blocks), (5, 0))
    else:
        arrays = gathered(rows, "replica") + gathered(acts, "replica")
        rows_at = tuple((i, 0) for i in range(groups))
        acts_at = tuple((groups + i, 0) for i in range(groups))
    total = group * groups
    slots = divisor_up_to(slot_count, SLOTS_PER_STEP)
    grads = call(
        functools.partial(grads_kernel, grid, rows_at, acts_at),
        [shape(gate_blocks.shape, bf16)] * 3,
        [gate_ids, up_ids, down_ids, *arrays],
        3,
        [
            pltpu.VMEM((row_count + 1, block, total), bf16),
            pltpu.VMEM((row_count + 1, total, block), bf16),
            pltpu.VMEM((col_count, block, total), bf16),
            pltpu.VMEM((col_count, total, block), bf16),
            pltpu.VMEM((col_count, total, block), bf16),
        ]
        + [pltpu.VMEM((slot_count, block, block), bf16)] * 3
        + [pltpu.SemaphoreType.DMA((3, slot_count // slots))],
        44,
        3 * step_flops * groups,
        out_hbm=True,
    )
    pieces, grads = lax.optimization_barrier((scattered(pieces, "tile"), grads))
    output, input_grad = (
        sum(piece[half].astype(f32) for piece in pieces).astype(bf16)
        for half in (slice(height), slice(height, None))
    )
    return (output, input_grad, *grads)


def solution(mesh):
    rows = P(("tile", "replica"), "dp")
    blocks = P("dp", "tile", None, None, None)
    ids = P("dp", "tile", None)
    return jax.shard_map(
        on_device,
        mesh=mesh,
        in_specs=(rows, rows, blocks, blocks, blocks, ids, ids, ids),
        out_specs=(rows, rows, blocks, blocks, blocks),
        check_vma=False,
    )
```

```python
import functools

import jax
import jax.numpy as jnp
from jax import lax
from jax.experimental import pallas as pl
from jax.experimental.pallas import tpu as pltpu
from jax.sharding import PartitionSpec as P

FF = 14336
SLOTS_PER_STEP = 32
MIB = 1 << 20


def divisor_up_to(count, limit):
    return max(step for step in range(1, limit + 1) if count % step == 0)


def place(slot_id, row_count, col_count):
    factor = -(-(1 << 16) // col_count)
    assert all((i * factor) >> 16 == i // col_count for i in range(row_count * col_count + 1))
    row = (slot_id * factor) >> 16
    return row, slot_id - row * col_count


def turned_scratch(blocks, count):
    slots = divisor_up_to(blocks.shape[2] // 2, SLOTS_PER_STEP)
    return [pltpu.VMEM((slots,) + blocks.shape[3:], blocks.dtype)] * (2 * count)


def streams(blocks, held, sems):
    slots = held[0].shape[0] // sems.shape[1]

    def copies(step):
        chunk = pl.ds(step * slots, slots)
        return [
            pltpu.make_async_copy(source.at[0, 0, chunk], target.at[chunk], sems.at[i, step])
            for i, (source, target) in enumerate(zip(blocks, held))
        ]

    return copies


def start_all(copies, steps):
    @pl.loop(0, steps)
    def _(step):
        for copy in copies(step):
            copy.start()


def over_slots(slot_count, steps, copies, body):
    slots = slot_count // steps

    @pl.loop(0, steps)
    def _(step):
        for copy in copies(step):
            copy.wait()
        for slot in range(slots):
            body(step * slots + slot)


def over_turned_slots(held, turned, steps, copies, body):
    assert steps % 2 == 0
    slots = held[0].shape[0] // steps

    def turn(step, slot, half):
        for source, targets in zip(held, turned):
            targets[half][slot] = source[step * slots + slot].T

    for copy in copies(0):
        copy.wait()
    for slot in range(slots):
        turn(0, slot, 0)

    @pl.loop(0, steps // 2)
    def _(pair):
        for half in range(2):
            step = 2 * pair + half
            later = jnp.minimum(step + 1, steps - 1)

            @pl.when(step + 1 < steps)
            def _():
                for copy in copies(later):
                    copy.wait()

            for slot in range(slots):
                body(step * slots + slot, [targets[half].at[slot] for targets in turned])
                turn(later, slot, 1 - half)


def filled_steps(ids, grid, steps, least=0):
    slot_count = ids.shape[-1]
    ends = lax.broadcasted_iota(jnp.int32, ids.shape, 2) + 1
    last = jnp.max(jnp.where(ids[...] < grid[0] * grid[1], ends, 0).astype(jnp.float32))
    slots = slot_count // steps
    return jnp.clip(lax.div(last.astype(jnp.int32) + (slots - 1), slots), least, steps)


def each(start, stop, body):
    lax.fori_loop(start, stop, lambda step, carry: (body(step), carry)[1], 0)


def stream_scratch(blocks, count, halves=1, limit=SLOTS_PER_STEP):
    slot_count, block = blocks.shape[2], blocks.shape[-1]
    steps = halves * (slot_count // halves // divisor_up_to(slot_count // halves, limit))
    return [pltpu.VMEM((slot_count, block, block), blocks.dtype)] * count + [
        pltpu.SemaphoreType.DMA((count, steps))
    ]


def in_hbm(value):
    return pltpu.with_memory_space_constraint(value, pltpu.HBM)


def call(kernel, out_shape, args, smem, scratch, vmem_mib, flops, out_hbm=False, fetched=0):
    ahead = smem + fetched
    memory = [
        pl.ANY if i < ahead or a.ndim == 5 else pltpu.VMEM for i, a in enumerate(args)
    ]
    args = [in_hbm(a) if i < ahead else a for i, a in enumerate(args)]
    inner = kernel

    def kernel(*refs):
        held, sems = refs[-1 - ahead : -1], refs[-1]
        copies = [
            pltpu.make_async_copy(ids, target, sems.at[i])
            for i, (ids, target) in enumerate(zip(refs[:ahead], held))
        ]
        for copy in copies:
            copy.start()

        def arrive():
            for copy in copies:
                copy.wait()

        inner(arrive, *held, *refs[ahead : -1 - ahead])

    if ahead:
        scratch = scratch + [pltpu.SMEM(a.shape, a.dtype) for a in args[:smem]]
        scratch += [pltpu.VMEM(a.shape, a.dtype) for a in args[smem:ahead]]
        scratch += [pltpu.SemaphoreType.DMA((ahead,))]
    else:
        kernel = inner
    size = sum(a.size * a.dtype.itemsize for a in jax.tree.leaves(out_shape))
    return pl.pallas_call(
        kernel,
        out_shape=out_shape,
        in_specs=[pl.BlockSpec(memory_space=space) for space in memory],
        out_specs=jax.tree.map(
            lambda _: pl.BlockSpec(memory_space=pl.ANY if out_hbm else pltpu.VMEM), out_shape
        ),
        scratch_shapes=scratch,
        compiler_params=pltpu.CompilerParams(vmem_limit_bytes=vmem_mib * MIB),
        cost_estimate=pl.CostEstimate(
            flops=20 * flops,
            bytes_accessed=size + sum(a.size * a.dtype.itemsize for a in args),
            transcendentals=0,
        ),
    )(*args)


def product(left, right):
    return jnp.dot(left, right, preferred_element_type=jnp.float32)


def zero(ref):
    ref[...] = jnp.zeros(ref.shape, ref.dtype)


def block_of(parts, row):
    return jnp.concatenate([part[:, row * 128 : (row + 1) * 128] for part in parts], axis=0)


def gate_up_kernel(grid, arrive, gate_ids, up_ids, gate_list, up_list, *refs):
    row_count, col_count = grid
    parts = refs[:-9]
    gate, up, out, source, gate_sum, up_sum, gate_held, up_held, sems = refs[-9:]
    copies = streams((gate, up), (gate_held, up_held), sems)
    steps = sems.shape[1]
    slots = gate_held.shape[0] // steps
    ahead = min(2, steps)
    for step in range(ahead):
        for copy in copies(step):
            copy.start()
    zero(source.at[row_count])
    zero(gate_sum)
    zero(up_sum)
    arrive()
    filled = [filled_steps(ids, grid, steps, ahead) for ids in (gate_list, up_list)]
    both = jnp.minimum(*filled)
    each(ahead, both, lambda step: [copy.start() for copy in copies(step)])
    for which in (0, 1):
        each(jnp.maximum(both, ahead), filled[which], lambda step, i=which: copies(step)[i].start())
    for row in range(row_count):
        source[row] = block_of(parts, row)
    matrices = ((gate_ids, gate_held, gate_sum), (up_ids, up_held, up_sum))

    def run(step, chosen):
        for which in chosen:
            copies(step)[which].wait()
        for index in range(slots):
            slot = step * slots + index
            for ids, held, total in (matrices[which] for which in chosen):
                row, col = place(ids[0, 0, slot], *grid)
                total[col] += product(source[row], held[slot])

    each(0, both, lambda step: run(step, (0, 1)))
    for which in (0, 1):
        each(both, filled[which], lambda step, i=which: run(step, (i,)))
    out[0] = gate_sum[...].astype(out.dtype)
    out[1] = up_sum[...].astype(out.dtype)


def rows_kernel(row_count, *refs):
    *parts, out = refs
    half = len(parts) // 2
    for row in range(row_count):
        out[row] = block_of(parts[:half], row)
        out[row_count + row] = block_of(parts[half:], row)
    zero(out.at[2 * row_count])


def back_kernel(grid, arrive, ids, rows, down, out, total, near, far, held, sems):
    row_count, col_count = grid
    copies = streams((down,), (held,), sems)
    start_all(copies, sems.shape[1])
    zero(total)
    arrive()

    def body(slot, turned):
        row, col = place(ids[0, 0, slot], *grid)
        total[col] += product(rows[row_count + row], turned[0][...])

    over_turned_slots((held,), ((near, far),), sems.shape[1], copies, body)
    out[...] = total[...].astype(out.dtype)


def gate_and_up(parts, col):
    return [sum(part[which, col].astype(jnp.float32) for part in parts) for which in (0, 1)]


def hidden_kernel(col_count, summands, row_arrays, row_blocks, *refs):
    parts, backs = refs[:summands], refs[summands : 2 * summands]
    rows = refs[2 * summands : 2 * summands + row_arrays]
    acts, *packs = refs[2 * summands + row_arrays :]
    for col in range(col_count):
        gate_sum, up_sum = gate_and_up(parts, col)
        grad = sum(back[col].astype(jnp.float32) for back in backs)
        sigmoid = jax.nn.sigmoid(gate_sum)
        silu_gate = gate_sum * sigmoid
        acts[col] = (silu_gate * up_sum).astype(acts.dtype)
        acts[col_count + col] = (
            grad * up_sum * sigmoid * (1.0 + gate_sum * (1.0 - sigmoid))
        ).astype(acts.dtype)
        acts[2 * col_count + col] = (grad * silu_gate).astype(acts.dtype)
    for pack in packs:
        for place_of, held in enumerate(rows):
            pack[place_of * row_blocks : (place_of + 1) * row_blocks] = held[:row_blocks]
        pack[len(rows) * row_blocks :] = acts[...]


def model_kernel(grid, arrive, gate_ids, up_ids, down_ids, acts, gate, up, down, *refs):
    row_count, col_count = grid
    *outs, y_sum, x_sum, gate_near, gate_far, up_near, up_far = refs[:-4]
    gate_held, up_held, down_held, sems = refs[-4:]
    copies = streams((gate, up, down), (gate_held, up_held, down_held), sems)
    start_all(copies, sems.shape[1])
    zero(y_sum)
    zero(x_sum)
    arrive()

    def body(slot, turned):
        for ids, blocks, which in ((gate_ids, turned[0], 1), (up_ids, turned[1], 2)):
            row, col = place(ids[0, 0, slot], *grid)
            x_sum[row] += product(acts[which * col_count + col], blocks[...])
        row, col = place(down_ids[0, 0, slot], *grid)
        y_sum[row] += product(acts[col], down_held[slot])

    halves = ((gate_near, gate_far), (up_near, up_far))
    over_turned_slots((gate_held, up_held), halves, sems.shape[1], copies, body)
    height = outs[0].shape[0] // 2
    for piece, out in enumerate(outs):
        tokens = slice(piece * height, (piece + 1) * height)
        for row in range(row_count):
            columns = slice(row * 128, (row + 1) * 128)
            out[:height, columns] = y_sum[row, tokens].astype(out.dtype)
            out[height:, columns] = x_sum[row, tokens].astype(out.dtype)


def grads_kernel(grid, rows, acts, arrive, gate_ids, up_ids, down_ids, *refs):
    lists, refs = refs[:3], refs[3:]
    row_count, col_count = grid
    gate_out, up_out, down_out, x, g, hidden, gate_act, up_act = refs[-13:-5]
    gate_buf, up_buf, down_buf, nothing, sems = refs[-5:]

    def joined(groups, index):
        return jnp.concatenate([refs[array][first + index] for array, first in groups], axis=0)

    slot_count = gate_buf.shape[0]
    slots = divisor_up_to(slot_count, SLOTS_PER_STEP)
    steps = slot_count // slots
    pairs = ((gate_buf, gate_out), (up_buf, up_out), (down_buf, down_out))

    def copy(which, step, empty=False):
        buf, out = pairs[which]
        chunk = pl.ds(step * slots, slots)
        source = nothing if empty else buf.at[chunk]
        return pltpu.make_async_copy(source, out.at[0, 0, chunk], sems.at[which, step])

    zero(nothing)
    arrive()
    filled = [filled_steps(ids, grid, steps) for ids in lists]
    for which in range(3):
        each(filled[which], steps, lambda step, i=which: copy(i, step, True).start())
    for row in range(row_count):
        x[row] = joined(rows, row).T
        g[row] = joined(rows, row_count + row)
    zero(x.at[row_count])
    zero(g.at[row_count])
    for col in range(col_count):
        hidden[col] = joined(acts, col).T
        gate_act[col] = joined(acts, col_count + col)
        up_act[col] = joined(acts, 2 * col_count + col)
    matrices = (
        (gate_ids, x, gate_act, gate_buf),
        (up_ids, x, up_act, up_buf),
        (down_ids, g, hidden, down_buf),
    )

    def run(step, chosen):
        for which in chosen:
            ids, model, act, buf = matrices[which]
            for index in range(slots):
                slot = step * slots + index
                row, col = place(ids[0, 0, slot], *grid)
                left, right = (act[col], model[row]) if which == 2 else (model[row], act[col])
                buf[slot] = product(left, right).astype(buf.dtype)
        for which in chosen:
            copy(which, step).start()

    every = jnp.minimum(jnp.minimum(*filled[:2]), filled[2])
    each(0, every, lambda step: run(step, (0, 1, 2)))
    for which in range(3):
        each(every, filled[which], lambda step, i=which: run(step, (i,)))
    for which in range(3):
        each(0, steps, lambda step, i=which: copy(i, step).wait())


def sent(value, axis, target):
    size = lax.axis_size(axis)
    return lax.ppermute(value, axis, [(i, target(i, size)) for i in range(size)])


def beyond(device, distance, size):
    return (device + distance) % size if size & (size - 1) else device ^ distance


def gathered(value, axis):
    size = lax.axis_size(axis)
    return [value] + [
        sent(value, axis, lambda i, n, d=d: beyond(i, d, n)) for d in range(1, size)
    ]


def across(value, distance):
    return sent(value, "replica", lambda i, n: i ^ distance)


def scattered(pieces, axis):
    size = lax.axis_size(axis)
    sign = -1 if size & (size - 1) else 1
    return [pieces[0]] + [
        sent(pieces[d], axis, lambda i, n, d=d: beyond(i, sign * d, n)) for d in range(1, size)
    ]


def on_device(tokens, out_grad, gate_blocks, up_blocks, down_blocks, gate_ids, up_ids, down_ids):
    slot_count, block = gate_blocks.shape[2], gate_blocks.shape[-1]
    tile, groups = lax.axis_size("tile"), lax.axis_size("replica")
    height = tokens.shape[0]
    group = height * tile
    row_count = tokens.shape[1] // block
    col_count = FF // tile // block
    grid = (row_count, col_count)
    bf16, f32 = jnp.bfloat16, jnp.float32
    shape = jax.ShapeDtypeStruct
    step_flops = 2 * slot_count * group * block * block

    token_parts, grad_parts = gathered(tokens, "tile"), gathered(out_grad, "tile")
    gate_up = call(
        functools.partial(gate_up_kernel, grid),
        shape((2, col_count, group, block), bf16),
        [gate_ids, up_ids, gate_ids, up_ids, *token_parts, gate_blocks, up_blocks],
        2,
        [pltpu.VMEM((row_count + 1, group, block), bf16)]
        + [pltpu.VMEM((col_count, group, block), f32)] * 2
        + stream_scratch(gate_blocks, 2, limit=48),
        48,
        2 * step_flops,
        fetched=3,
    )
    _, grad_parts = lax.optimization_barrier((gate_up, grad_parts))
    rows = call(
        functools.partial(rows_kernel, row_count),
        shape((2 * row_count + 1, group, block), bf16),
        [*token_parts, *grad_parts],
        0,
        [],
        8,
        1,
    )
    packed = groups == 4
    far_rows = across(rows, 2) if packed else None
    back = call(
        functools.partial(back_kernel, grid),
        shape((col_count, group, block), bf16),
        [down_ids, rows, down_blocks],
        1,
        [
            pltpu.VMEM((col_count, group, block), f32),
            *turned_scratch(down_blocks, 1),
            *stream_scratch(down_blocks, 1, 2),
        ],
        48,
        step_flops,
    )
    gate_up_parts = gathered(gate_up, "dp")
    gate_up_parts, _ = lax.optimization_barrier((gate_up_parts, back))
    back_parts, far_rows = lax.optimization_barrier((gathered(back, "dp"), far_rows))
    acts_shape = shape((3 * col_count, group, block), bf16)
    row_blocks = 2 * row_count
    pack_shape = shape((2 * row_blocks + 3 * col_count, group, block), bf16)
    acts, *pack = call(
        functools.partial(hidden_kernel, col_count, len(back_parts), 2 * packed, row_blocks),
        [acts_shape, pack_shape] if packed else [acts_shape],
        [*gate_up_parts, *back_parts, *([rows, far_rows] if packed else [])],
        0,
        [],
        8,
        1,
    )
    far_acts = across(acts, 2) if packed else None
    pieces = call(
        functools.partial(model_kernel, grid),
        [shape((2 * height, row_count * block), bf16)] * tile,
        [gate_ids, up_ids, down_ids, acts, gate_blocks, up_blocks, down_blocks],
        3,
        [pltpu.VMEM((row_count + 1, group, block), f32)] * 2
        + [*turned_scratch(gate_blocks, 2), *stream_scratch(gate_blocks, 3, 2)],
        48,
        3 * step_flops,
    )
    if packed:
        _, far_acts = lax.optimization_barrier((pieces, far_acts))
        arrays = [rows, far_rows, across(pack[0], 1), acts, far_acts, across(far_acts, 1)]
        rows_at = ((0, 0), (1, 0), (2, 0), (2, row_blocks))
        acts_at = ((3, 0), (4, 0), (2, 2 * row_blocks), (5, 0))
    else:
        arrays = gathered(rows, "replica") + gathered(acts, "replica")
        rows_at = tuple((i, 0) for i in range(groups))
        acts_at = tuple((groups + i, 0) for i in range(groups))
    total = group * groups
    slots = divisor_up_to(slot_count, SLOTS_PER_STEP)
    grads = call(
        functools.partial(grads_kernel, grid, rows_at, acts_at),
        [shape(gate_blocks.shape, bf16)] * 3,
        [gate_ids, up_ids, down_ids, gate_ids, up_ids, down_ids, *arrays],
        3,
        [
            pltpu.VMEM((row_count + 1, block, total), bf16),
            pltpu.VMEM((row_count + 1, total, block), bf16),
            pltpu.VMEM((col_count, block, total), bf16),
            pltpu.VMEM((col_count, total, block), bf16),
            pltpu.VMEM((col_count, total, block), bf16),
        ]
        + [pltpu.VMEM((slot_count, block, block), bf16)] * 3
        + [
            pltpu.VMEM((slots, block, block), bf16),
            pltpu.SemaphoreType.DMA((3, slot_count // slots)),
        ],
        46,
        3 * step_flops * groups,
        out_hbm=True,
        fetched=3,
    )
    pieces, grads = lax.optimization_barrier((scattered(pieces, "tile"), grads))
    output, input_grad = (
        sum(piece[half].astype(f32) for piece in pieces).astype(bf16)
        for half in (slice(height), slice(height, None))
    )
    return (output, input_grad, *grads)


def solution(mesh):
    rows = P(("tile", "replica"), "dp")
    blocks = P("dp", "tile", None, None, None)
    ids = P("dp", "tile", None)
    return jax.shard_map(
        on_device,
        mesh=mesh,
        in_specs=(rows, rows, blocks, blocks, blocks, ids, ids, ids),
        out_specs=(rows, rows, blocks, blocks, blocks),
        check_vma=False,
    )
```

```python
import functools

import jax
import jax.numpy as jnp
from jax import lax
from jax.experimental import pallas as pl
from jax.experimental.pallas import tpu as pltpu
from jax.sharding import PartitionSpec as P

FF = 14336
SLOTS_PER_STEP = 32
MIB = 1 << 20


def divisor_up_to(count, limit):
    return max(step for step in range(1, limit + 1) if count % step == 0)


def place(slot_id, row_count, col_count):
    factor = -(-(1 << 16) // col_count)
    assert all((i * factor) >> 16 == i // col_count for i in range(row_count * col_count + 1))
    row = (slot_id * factor) >> 16
    return row, slot_id - row * col_count


def turned_scratch(blocks, count):
    slots = divisor_up_to(blocks.shape[2] // 2, SLOTS_PER_STEP)
    return [pltpu.VMEM((slots,) + blocks.shape[3:], blocks.dtype)] * (2 * count)


def streams(blocks, held, sems):
    slots = held[0].shape[0] // sems.shape[1]

    def copies(step):
        chunk = pl.ds(step * slots, slots)
        return [
            pltpu.make_async_copy(source.at[0, 0, chunk], target.at[chunk], sems.at[i, step])
            for i, (source, target) in enumerate(zip(blocks, held))
        ]

    return copies


def start_all(copies, steps):
    @pl.loop(0, steps)
    def _(step):
        for copy in copies(step):
            copy.start()


def over_slots(slot_count, steps, copies, body):
    slots = slot_count // steps

    @pl.loop(0, steps)
    def _(step):
        for copy in copies(step):
            copy.wait()
        for slot in range(slots):
            body(step * slots + slot)


def over_turned_slots(held, turned, steps, copies, body, filled=None):
    assert steps % 2 == 0
    slots = held[0].shape[0] // steps

    def turn(step, slot, half):
        for source, targets in zip(held, turned):
            targets[half][slot] = source[step * slots + slot].T

    for copy in copies(0):
        copy.wait()
    for slot in range(slots):
        turn(0, slot, 0)

    @pl.loop(0, steps // 2)
    def _(pair):
        for half in range(2):
            step = 2 * pair + half
            later = jnp.minimum(step + 1, steps - 1)

            for copy, stop in zip(copies(later), filled or [steps] * len(held)):
                pl.when(step + 1 < stop)(copy.wait)

            for slot in range(slots):
                body(step * slots + slot, [targets[half].at[slot] for targets in turned])
                turn(later, slot, 1 - half)


def filled_steps(ids, grid, steps, least=0):
    slot_count = ids.shape[-1]
    ends = lax.broadcasted_iota(jnp.int32, ids.shape, 2) + 1
    last = jnp.max(jnp.where(ids[...] < grid[0] * grid[1], ends, 0).astype(jnp.float32))
    slots = slot_count // steps
    return jnp.clip(lax.div(last.astype(jnp.int32) + (slots - 1), slots), least, steps)


def each(start, stop, body):
    lax.fori_loop(start, stop, lambda step, carry: (body(step), carry)[1], 0)


def stream_scratch(blocks, count, halves=1, limit=SLOTS_PER_STEP):
    slot_count, block = blocks.shape[2], blocks.shape[-1]
    steps = halves * (slot_count // halves // divisor_up_to(slot_count // halves, limit))
    return [pltpu.VMEM((slot_count, block, block), blocks.dtype)] * count + [
        pltpu.SemaphoreType.DMA((count, steps))
    ]


def in_hbm(value):
    return pltpu.with_memory_space_constraint(value, pltpu.HBM)


def call(kernel, out_shape, args, smem, scratch, vmem_mib, flops, out_hbm=False, fetched=0):
    ahead = smem + fetched
    memory = [
        pl.ANY if i < ahead or a.ndim == 5 else pltpu.VMEM for i, a in enumerate(args)
    ]
    args = [in_hbm(a) if i < ahead else a for i, a in enumerate(args)]
    inner = kernel

    def kernel(*refs):
        held, sems = refs[-1 - ahead : -1], refs[-1]
        copies = [
            pltpu.make_async_copy(ids, target, sems.at[i])
            for i, (ids, target) in enumerate(zip(refs[:ahead], held))
        ]
        for copy in copies:
            copy.start()

        def arrive():
            for copy in copies:
                copy.wait()

        inner(arrive, *held, *refs[ahead : -1 - ahead])

    if ahead:
        scratch = scratch + [pltpu.SMEM(a.shape, a.dtype) for a in args[:smem]]
        scratch += [pltpu.VMEM(a.shape, a.dtype) for a in args[smem:ahead]]
        scratch += [pltpu.SemaphoreType.DMA((ahead,))]
    else:
        kernel = inner
    size = sum(a.size * a.dtype.itemsize for a in jax.tree.leaves(out_shape))
    return pl.pallas_call(
        kernel,
        out_shape=out_shape,
        in_specs=[pl.BlockSpec(memory_space=space) for space in memory],
        out_specs=jax.tree.map(
            lambda _: pl.BlockSpec(memory_space=pl.ANY if out_hbm else pltpu.VMEM), out_shape
        ),
        scratch_shapes=scratch,
        compiler_params=pltpu.CompilerParams(vmem_limit_bytes=vmem_mib * MIB),
        cost_estimate=pl.CostEstimate(
            flops=20 * flops,
            bytes_accessed=size + sum(a.size * a.dtype.itemsize for a in args),
            transcendentals=0,
        ),
    )(*args)


def product(left, right):
    return jnp.dot(left, right, preferred_element_type=jnp.float32)


def zero(ref):
    ref[...] = jnp.zeros(ref.shape, ref.dtype)


def block_of(parts, row):
    return jnp.concatenate([part[:, row * 128 : (row + 1) * 128] for part in parts], axis=0)


def gate_up_kernel(grid, arrive, gate_ids, up_ids, gate_list, up_list, *refs):
    row_count, col_count = grid
    parts = refs[:-9]
    gate, up, out, source, gate_sum, up_sum, gate_held, up_held, sems = refs[-9:]
    copies = streams((gate, up), (gate_held, up_held), sems)
    steps = sems.shape[1]
    slots = gate_held.shape[0] // steps
    ahead = min(2, steps)
    for step in range(ahead):
        for copy in copies(step):
            copy.start()
    zero(source.at[row_count])
    zero(gate_sum)
    zero(up_sum)
    arrive()
    filled = [filled_steps(ids, grid, steps, ahead) for ids in (gate_list, up_list)]
    both = jnp.minimum(*filled)
    each(ahead, both, lambda step: [copy.start() for copy in copies(step)])
    for which in (0, 1):
        each(jnp.maximum(both, ahead), filled[which], lambda step, i=which: copies(step)[i].start())
    for row in range(row_count):
        source[row] = block_of(parts, row)
    matrices = ((gate_ids, gate_held, gate_sum), (up_ids, up_held, up_sum))

    def run(step, chosen):
        for which in chosen:
            copies(step)[which].wait()
        for index in range(slots):
            slot = step * slots + index
            for ids, held, total in (matrices[which] for which in chosen):
                row, col = place(ids[0, 0, slot], *grid)
                total[col] += product(source[row], held[slot])

    each(0, both, lambda step: run(step, (0, 1)))
    for which in (0, 1):
        each(both, filled[which], lambda step, i=which: run(step, (i,)))
    out[0] = gate_sum[...].astype(out.dtype)
    out[1] = up_sum[...].astype(out.dtype)


def rows_kernel(row_count, *refs):
    *parts, out = refs
    half = len(parts) // 2
    for row in range(row_count):
        out[row] = block_of(parts[:half], row)
        out[row_count + row] = block_of(parts[half:], row)
    zero(out.at[2 * row_count])


def back_kernel(grid, arrive, ids, rows, down, out, total, near, far, held, sems):
    row_count, col_count = grid
    copies = streams((down,), (held,), sems)
    start_all(copies, sems.shape[1])
    zero(total)
    arrive()

    def body(slot, turned):
        row, col = place(ids[0, 0, slot], *grid)
        total[col] += product(rows[row_count + row], turned[0][...])

    over_turned_slots((held,), ((near, far),), sems.shape[1], copies, body)
    out[...] = total[...].astype(out.dtype)


def gate_and_up(parts, col):
    return [sum(part[which, col].astype(jnp.float32) for part in parts) for which in (0, 1)]


def hidden_kernel(col_count, *refs):
    *parts, out = refs
    for col in range(col_count):
        gate_sum, up_sum = gate_and_up(parts, col)
        out[col] = (gate_sum * jax.nn.sigmoid(gate_sum) * up_sum).astype(out.dtype)


def act_grads_kernel(col_count, summands, row_arrays, row_blocks, *refs):
    parts, backs = refs[:summands], refs[summands : 2 * summands]
    hidden = refs[2 * summands]
    rows = refs[2 * summands + 1 : 2 * summands + 1 + row_arrays]
    acts, *packs = refs[2 * summands + 1 + row_arrays :]
    for col in range(col_count):
        gate_sum, up_sum = gate_and_up(parts, col)
        grad = sum(back[col].astype(jnp.float32) for back in backs)
        sigmoid = jax.nn.sigmoid(gate_sum)
        silu_gate = gate_sum * sigmoid
        acts[col] = (grad * up_sum * sigmoid * (1.0 + gate_sum * (1.0 - sigmoid))).astype(
            acts.dtype
        )
        acts[col_count + col] = (grad * silu_gate).astype(acts.dtype)
    for pack in packs:
        first = len(rows) * row_blocks
        for place_of, held in enumerate(rows):
            pack[place_of * row_blocks : (place_of + 1) * row_blocks] = held[:row_blocks]
        pack[first : first + col_count] = hidden[...]
        pack[first + col_count :] = acts[...]


def model_kernel(grid, arrive, gate_ids, up_ids, down_ids, *refs):
    row_count, col_count = grid
    lists, (hidden, acts, gate, up, down) = refs[:3], refs[3:8]
    refs = refs[8:]
    *outs, y_sum, x_sum, gate_near, gate_far, up_near, up_far = refs[:-4]
    gate_held, up_held, down_held, sems = refs[-4:]
    copies = streams((gate, up, down), (gate_held, up_held, down_held), sems)
    steps = sems.shape[1]
    for copy in copies(0):
        copy.start()
    zero(y_sum)
    zero(x_sum)
    arrive()
    filled = [filled_steps(ids, grid, steps, 1) for ids in lists]

    @pl.loop(1, steps)
    def _(step):
        for copy, stop in zip(copies(step), filled):
            pl.when(step < stop)(copy.start)

    def body(slot, turned):
        for ids, blocks, which in ((gate_ids, turned[0], 0), (up_ids, turned[1], 1)):
            row, col = place(ids[0, 0, slot], *grid)
            x_sum[row] += product(acts[which * col_count + col], blocks[...])
        row, col = place(down_ids[0, 0, slot], *grid)
        y_sum[row] += product(hidden[col], down_held[slot])

    halves = ((gate_near, gate_far), (up_near, up_far))
    over_turned_slots((gate_held, up_held), halves, steps, copies, body, filled)
    height = outs[0].shape[0] // 2
    for piece, out in enumerate(outs):
        tokens = slice(piece * height, (piece + 1) * height)
        for row in range(row_count):
            columns = slice(row * 128, (row + 1) * 128)
            out[:height, columns] = y_sum[row, tokens].astype(out.dtype)
            out[height:, columns] = x_sum[row, tokens].astype(out.dtype)


def grads_kernel(grid, rows, hiddens, acts, arrive, gate_ids, up_ids, down_ids, *refs):
    lists, refs = refs[:3], refs[3:]
    row_count, col_count = grid
    gate_out, up_out, down_out, x, g, hidden, gate_act, up_act = refs[-13:-5]
    gate_buf, up_buf, down_buf, nothing, sems = refs[-5:]

    def joined(groups, index):
        return jnp.concatenate([refs[array][first + index] for array, first in groups], axis=0)

    slot_count = gate_buf.shape[0]
    slots = divisor_up_to(slot_count, SLOTS_PER_STEP)
    steps = slot_count // slots
    pairs = ((gate_buf, gate_out), (up_buf, up_out), (down_buf, down_out))

    def copy(which, step, empty=False):
        buf, out = pairs[which]
        chunk = pl.ds(step * slots, slots)
        source = nothing if empty else buf.at[chunk]
        return pltpu.make_async_copy(source, out.at[0, 0, chunk], sems.at[which, step])

    zero(nothing)
    arrive()
    filled = [filled_steps(ids, grid, steps) for ids in lists]
    for which in range(3):
        each(filled[which], steps, lambda step, i=which: copy(i, step, True).start())
    for row in range(row_count):
        x[row] = joined(rows, row).T
        g[row] = joined(rows, row_count + row)
    zero(x.at[row_count])
    zero(g.at[row_count])
    for col in range(col_count):
        hidden[col] = joined(hiddens, col).T
        gate_act[col] = joined(acts, col)
        up_act[col] = joined(acts, col_count + col)
    matrices = (
        (gate_ids, x, gate_act, gate_buf),
        (up_ids, x, up_act, up_buf),
        (down_ids, g, hidden, down_buf),
    )

    def run(step, chosen):
        for which in chosen:
            ids, model, act, buf = matrices[which]
            for index in range(slots):
                slot = step * slots + index
                row, col = place(ids[0, 0, slot], *grid)
                left, right = (act[col], model[row]) if which == 2 else (model[row], act[col])
                buf[slot] = product(left, right).astype(buf.dtype)
        for which in chosen:
            copy(which, step).start()

    every = jnp.minimum(jnp.minimum(*filled[:2]), filled[2])
    each(0, every, lambda step: run(step, (0, 1, 2)))
    for which in range(3):
        each(every, filled[which], lambda step, i=which: run(step, (i,)))
    for which in range(3):
        each(0, steps, lambda step, i=which: copy(i, step).wait())


def sent(value, axis, target):
    size = lax.axis_size(axis)
    return lax.ppermute(value, axis, [(i, target(i, size)) for i in range(size)])


def beyond(device, distance, size):
    return (device + distance) % size if size & (size - 1) else device ^ distance


def gathered(value, axis):
    size = lax.axis_size(axis)
    return [value] + [
        sent(value, axis, lambda i, n, d=d: beyond(i, d, n)) for d in range(1, size)
    ]


def across(value, distance):
    return sent(value, "replica", lambda i, n: i ^ distance)


def scattered(pieces, axis):
    size = lax.axis_size(axis)
    sign = -1 if size & (size - 1) else 1
    return [pieces[0]] + [
        sent(pieces[d], axis, lambda i, n, d=d: beyond(i, sign * d, n)) for d in range(1, size)
    ]


def on_device(tokens, out_grad, gate_blocks, up_blocks, down_blocks, gate_ids, up_ids, down_ids):
    slot_count, block = gate_blocks.shape[2], gate_blocks.shape[-1]
    tile, groups = lax.axis_size("tile"), lax.axis_size("replica")
    height = tokens.shape[0]
    group = height * tile
    row_count = tokens.shape[1] // block
    col_count = FF // tile // block
    grid = (row_count, col_count)
    bf16, f32 = jnp.bfloat16, jnp.float32
    shape = jax.ShapeDtypeStruct
    step_flops = 2 * slot_count * group * block * block

    token_parts, grad_parts = gathered(tokens, "tile"), gathered(out_grad, "tile")
    gate_up = call(
        functools.partial(gate_up_kernel, grid),
        shape((2, col_count, group, block), bf16),
        [gate_ids, up_ids, gate_ids, up_ids, *token_parts, gate_blocks, up_blocks],
        2,
        [pltpu.VMEM((row_count + 1, group, block), bf16)]
        + [pltpu.VMEM((col_count, group, block), f32)] * 2
        + stream_scratch(gate_blocks, 2, limit=48),
        48,
        2 * step_flops,
        fetched=3,
    )
    _, grad_parts = lax.optimization_barrier((gate_up, grad_parts))
    rows = call(
        functools.partial(rows_kernel, row_count),
        shape((2 * row_count + 1, group, block), bf16),
        [*token_parts, *grad_parts],
        0,
        [],
        8,
        1,
    )
    packed = groups == 4
    far_rows = across(rows, 2) if packed else None
    back = call(
        functools.partial(back_kernel, grid),
        shape((col_count, group, block), bf16),
        [down_ids, rows, down_blocks],
        1,
        [
            pltpu.VMEM((col_count, group, block), f32),
            *turned_scratch(down_blocks, 1),
            *stream_scratch(down_blocks, 1, 2),
        ],
        48,
        step_flops,
    )
    gate_up_parts = gathered(gate_up, "dp")
    gate_up_parts, _ = lax.optimization_barrier((gate_up_parts, back))
    hidden = call(
        functools.partial(hidden_kernel, col_count),
        shape((col_count, group, block), bf16),
        gate_up_parts,
        0,
        [],
        8,
        1,
    )
    far_hidden = across(hidden, 2) if packed else None
    back_parts, far_rows, hidden = lax.optimization_barrier(
        (gathered(back, "dp"), far_rows, hidden)
    )
    acts_shape = shape((2 * col_count, group, block), bf16)
    row_blocks = 2 * row_count
    pack_shape = shape((2 * row_blocks + 3 * col_count, group, block), bf16)
    acts, *pack = call(
        functools.partial(act_grads_kernel, col_count, len(back_parts), 2 * packed, row_blocks),
        [acts_shape, pack_shape] if packed else [acts_shape],
        [*gate_up_parts, *back_parts, hidden, *([rows, far_rows] if packed else [])],
        0,
        [],
        8,
        1,
    )
    far_acts = across(acts, 2) if packed else None
    pieces = call(
        functools.partial(model_kernel, grid),
        [shape((2 * height, row_count * block), bf16)] * tile,
        [
            *[gate_ids, up_ids, down_ids] * 2,
            hidden,
            acts,
            gate_blocks,
            up_blocks,
            down_blocks,
        ],
        3,
        [pltpu.VMEM((row_count + 1, group, block), f32)] * 2
        + [*turned_scratch(gate_blocks, 2), *stream_scratch(gate_blocks, 3, 2)],
        48,
        3 * step_flops,
        fetched=3,
    )
    if packed:
        _, far_hidden, far_acts = lax.optimization_barrier((pieces, far_hidden, far_acts))
        arrays = [rows, far_rows, across(pack[0], 1), hidden, far_hidden, across(far_hidden, 1)]
        arrays += [acts, far_acts, across(far_acts, 1)]
        rows_at = ((0, 0), (1, 0), (2, 0), (2, row_blocks))
        hidden_at = ((3, 0), (4, 0), (2, 2 * row_blocks), (5, 0))
        acts_at = ((6, 0), (7, 0), (2, 2 * row_blocks + col_count), (8, 0))
    else:
        arrays = [piece for whole in (rows, hidden, acts) for piece in gathered(whole, "replica")]
        rows_at, hidden_at, acts_at = (
            tuple((first * groups + i, 0) for i in range(groups)) for first in range(3)
        )
    total = group * groups
    slots = divisor_up_to(slot_count, SLOTS_PER_STEP)
    grads = call(
        functools.partial(grads_kernel, grid, rows_at, hidden_at, acts_at),
        [shape(gate_blocks.shape, bf16)] * 3,
        [gate_ids, up_ids, down_ids, gate_ids, up_ids, down_ids, *arrays],
        3,
        [
            pltpu.VMEM((row_count + 1, block, total), bf16),
            pltpu.VMEM((row_count + 1, total, block), bf16),
            pltpu.VMEM((col_count, block, total), bf16),
            pltpu.VMEM((col_count, total, block), bf16),
            pltpu.VMEM((col_count, total, block), bf16),
        ]
        + [pltpu.VMEM((slot_count, block, block), bf16)] * 3
        + [
            pltpu.VMEM((slots, block, block), bf16),
            pltpu.SemaphoreType.DMA((3, slot_count // slots)),
        ],
        46,
        3 * step_flops * groups,
        out_hbm=True,
        fetched=3,
    )
    pieces, grads = lax.optimization_barrier((scattered(pieces, "tile"), grads))
    output, input_grad = (
        sum(piece[half].astype(f32) for piece in pieces).astype(bf16)
        for half in (slice(height), slice(height, None))
    )
    return (output, input_grad, *grads)


def solution(mesh):
    rows = P(("tile", "replica"), "dp")
    blocks = P("dp", "tile", None, None, None)
    ids = P("dp", "tile", None)
    return jax.shard_map(
        on_device,
        mesh=mesh,
        in_specs=(rows, rows, blocks, blocks, blocks, ids, ids, ids),
        out_specs=(rows, rows, blocks, blocks, blocks),
        check_vma=False,
    )
```

```python
import functools

import jax
import jax.numpy as jnp
from jax import lax
from jax.experimental import pallas as pl
from jax.experimental.pallas import tpu as pltpu
from jax.sharding import PartitionSpec as P

FF = 14336
SLOTS_PER_STEP = 32
MIB = 1 << 20


def divisor_up_to(count, limit):
    return max(step for step in range(1, limit + 1) if count % step == 0)


def place(slot_id, row_count, col_count):
    factor = -(-(1 << 16) // col_count)
    assert all((i * factor) >> 16 == i // col_count for i in range(row_count * col_count + 1))
    row = (slot_id * factor) >> 16
    return row, slot_id - row * col_count


def turned_scratch(blocks, count, parts=1):
    slots = divisor_up_to(blocks.shape[2] * parts // 2, SLOTS_PER_STEP) // parts
    return [pltpu.VMEM((slots,) + blocks.shape[3:], blocks.dtype)] * (2 * count)


def streams(blocks, held, sems):
    slots = held[0].shape[0] // sems.shape[1]

    def copies(step):
        chunk = pl.ds(step * slots, slots)
        return [
            pltpu.make_async_copy(source.at[0, 0, chunk], target.at[chunk], sems.at[i, step])
            for i, (source, target) in enumerate(zip(blocks, held))
        ]

    return copies


def start_all(copies, steps):
    @pl.loop(0, steps)
    def _(step):
        for copy in copies(step):
            copy.start()


def over_slots(slot_count, steps, copies, body):
    slots = slot_count // steps

    @pl.loop(0, steps)
    def _(step):
        for copy in copies(step):
            copy.wait()
        for slot in range(slots):
            body(step * slots + slot)


def over_turned_slots(held, turned, steps, copies, body):
    assert steps % 2 == 0
    slots = held[0].shape[0] // steps

    def turn(step, slot, half):
        for source, targets in zip(held, turned):
            targets[half][slot] = source[step * slots + slot].T

    for copy in copies(0):
        copy.wait()
    for slot in range(slots):
        turn(0, slot, 0)

    @pl.loop(0, steps // 2)
    def _(pair):
        for half in range(2):
            step = 2 * pair + half
            later = jnp.minimum(step + 1, steps - 1)

            @pl.when(step + 1 < steps)
            def _():
                for copy in copies(later):
                    copy.wait()

            for slot in range(slots):
                body(step * slots + slot, [targets[half].at[slot] for targets in turned])
                turn(later, slot, 1 - half)


def filled_steps(ids, grid, steps, least=0):
    slot_count = ids.shape[-1]
    ends = lax.broadcasted_iota(jnp.int32, ids.shape, 2) + 1
    last = jnp.max(jnp.where(ids[...] < grid[0] * grid[1], ends, 0).astype(jnp.float32))
    slots = slot_count // steps
    return jnp.clip(lax.div(last.astype(jnp.int32) + (slots - 1), slots), least, steps)


def each(start, stop, body):
    lax.fori_loop(start, stop, lambda step, carry: (body(step), carry)[1], 0)


def stream_scratch(blocks, count, halves=1, limit=SLOTS_PER_STEP):
    slot_count, block = blocks.shape[2], blocks.shape[-1]
    steps = halves * (slot_count // halves // divisor_up_to(slot_count // halves, limit))
    return [pltpu.VMEM((slot_count, block, block), blocks.dtype)] * count + [
        pltpu.SemaphoreType.DMA((count, steps))
    ]


def in_hbm(value):
    return pltpu.with_memory_space_constraint(value, pltpu.HBM)


def call(kernel, out_shape, args, smem, scratch, vmem_mib, flops, out_hbm=False, fetched=0):
    ahead = smem + fetched
    memory = [
        pl.ANY if i < ahead or a.ndim == 5 else pltpu.VMEM for i, a in enumerate(args)
    ]
    args = [in_hbm(a) if i < ahead else a for i, a in enumerate(args)]
    inner = kernel

    def kernel(*refs):
        held, sems = refs[-1 - ahead : -1], refs[-1]
        copies = [
            pltpu.make_async_copy(ids, target, sems.at[i])
            for i, (ids, target) in enumerate(zip(refs[:ahead], held))
        ]
        for copy in copies:
            copy.start()

        def arrive():
            for copy in copies:
                copy.wait()

        inner(arrive, *held, *refs[ahead : -1 - ahead])

    if ahead:
        scratch = scratch + [pltpu.SMEM(a.shape, a.dtype) for a in args[:smem]]
        scratch += [pltpu.VMEM(a.shape, a.dtype) for a in args[smem:ahead]]
        scratch += [pltpu.SemaphoreType.DMA((ahead,))]
    else:
        kernel = inner
    size = sum(a.size * a.dtype.itemsize for a in jax.tree.leaves(out_shape))
    return pl.pallas_call(
        kernel,
        out_shape=out_shape,
        in_specs=[pl.BlockSpec(memory_space=space) for space in memory],
        out_specs=jax.tree.map(
            lambda _: pl.BlockSpec(memory_space=pl.ANY if out_hbm else pltpu.VMEM), out_shape
        ),
        scratch_shapes=scratch,
        compiler_params=pltpu.CompilerParams(vmem_limit_bytes=vmem_mib * MIB),
        cost_estimate=pl.CostEstimate(
            flops=20 * flops,
            bytes_accessed=size + sum(a.size * a.dtype.itemsize for a in args),
            transcendentals=0,
        ),
    )(*args)


def product(left, right):
    return jnp.dot(left, right, preferred_element_type=jnp.float32)


def zero(ref):
    ref[...] = jnp.zeros(ref.shape, ref.dtype)


def block_of(parts, row):
    return jnp.concatenate([part[:, row * 128 : (row + 1) * 128] for part in parts], axis=0)


def gate_up_kernel(grid, arrive, gate_ids, up_ids, gate_list, up_list, *refs):
    row_count, col_count = grid
    parts = refs[:-9]
    gate, up, out, source, gate_sum, up_sum, gate_held, up_held, sems = refs[-9:]
    copies = streams((gate, up), (gate_held, up_held), sems)
    steps = sems.shape[1]
    slots = gate_held.shape[0] // steps
    ahead = min(2, steps)
    for step in range(ahead):
        for copy in copies(step):
            copy.start()
    zero(source.at[row_count])
    zero(gate_sum)
    zero(up_sum)
    arrive()
    filled = [filled_steps(ids, grid, steps, ahead) for ids in (gate_list, up_list)]
    both = jnp.minimum(*filled)
    each(ahead, both, lambda step: [copy.start() for copy in copies(step)])
    for which in (0, 1):
        each(jnp.maximum(both, ahead), filled[which], lambda step, i=which: copies(step)[i].start())
    for row in range(row_count):
        source[row] = block_of(parts, row)
    matrices = ((gate_ids, gate_held, gate_sum), (up_ids, up_held, up_sum))

    def run(step, chosen):
        for which in chosen:
            copies(step)[which].wait()
        for index in range(slots):
            slot = step * slots + index
            for ids, held, total in (matrices[which] for which in chosen):
                row, col = place(ids[0, 0, slot], *grid)
                total[col] += product(source[row], held[slot])

    each(0, both, lambda step: run(step, (0, 1)))
    for which in (0, 1):
        each(both, filled[which], lambda step, i=which: run(step, (i,)))
    out[0] = gate_sum[...].astype(out.dtype)
    out[1] = up_sum[...].astype(out.dtype)


def rows_kernel(row_count, *refs):
    *parts, out = refs
    half = len(parts) // 2
    for row in range(row_count):
        out[row] = block_of(parts[:half], row)
        out[row_count + row] = block_of(parts[half:], row)
    zero(out.at[2 * row_count])


def back_kernel(grid, arrive, ids, rows, down, out, total, near, far, held, sems):
    row_count, col_count = grid
    copies = streams((down,), (held,), sems)
    start_all(copies, sems.shape[1])
    zero(total)
    arrive()

    def body(slot, turned):
        row, col = place(ids[0, 0, slot], *grid)
        total[col] += product(rows[row_count + row], turned[0][...])

    over_turned_slots((held,), ((near, far),), sems.shape[1], copies, body)
    out[...] = total[...].astype(out.dtype)


def gate_and_up(parts, col):
    return [sum(part[which, col].astype(jnp.float32) for part in parts) for which in (0, 1)]


def hidden_kernel(col_count, *refs):
    *parts, out = refs
    for col in range(col_count):
        gate_sum, up_sum = gate_and_up(parts, col)
        out[col] = (gate_sum * jax.nn.sigmoid(gate_sum) * up_sum).astype(out.dtype)


def act_grads_kernel(col_count, summands, row_arrays, row_blocks, *refs):
    parts, backs = refs[:summands], refs[summands : 2 * summands]
    hidden = refs[2 * summands]
    rows = refs[2 * summands + 1 : 2 * summands + 1 + row_arrays]
    acts, *packs = refs[2 * summands + 1 + row_arrays :]
    for col in range(col_count):
        gate_sum, up_sum = gate_and_up(parts, col)
        grad = sum(back[col].astype(jnp.float32) for back in backs)
        sigmoid = jax.nn.sigmoid(gate_sum)
        silu_gate = gate_sum * sigmoid
        acts[col] = (grad * up_sum * sigmoid * (1.0 + gate_sum * (1.0 - sigmoid))).astype(
            acts.dtype
        )
        acts[col_count + col] = (grad * silu_gate).astype(acts.dtype)
    for pack in packs:
        first = len(rows) * row_blocks
        for place_of, held in enumerate(rows):
            pack[place_of * row_blocks : (place_of + 1) * row_blocks] = held[:row_blocks]
        pack[first : first + col_count] = hidden[...]
        pack[first + col_count :] = acts[...]


def model_kernel(grid, arrive, gate_ids, up_ids, down_ids, *refs):
    row_count, col_count = grid
    lists, (hidden, acts, gate, up, down) = refs[:3], refs[3:8]
    *outs, y_sum, x_sum, gate_near, gate_far, up_near, up_far = refs[8:-4]
    gate_held, up_held, down_held, sems = refs[-4:]
    copies = streams((gate, up, down), (gate_held, up_held, down_held), sems)
    steps = sems.shape[1]
    slots = gate_held.shape[0] // steps
    half = slots // 2
    for copy in copies(0):
        copy.start()
    zero(y_sum)
    zero(x_sum)
    arrive()
    filled = [filled_steps(ids, grid, steps, 1) for ids in lists]

    @pl.loop(1, steps)
    def _(step):
        for copy, stop in zip(copies(step), filled):
            pl.when(step < stop)(copy.start)

    matrices = (
        (gate_ids, gate_held, (gate_near, gate_far)),
        (up_ids, up_held, (up_near, up_far)),
        (down_ids, down_held, None),
    )

    def turn(which, step, index):
        _, held, halves = matrices[which]
        halves[index // half][index % half] = held[step * slots + index].T

    def multiply(which, step, index):
        ids, held, halves = matrices[which]
        slot = step * slots + index
        row, col = place(ids[0, 0, slot], *grid)
        if which == 2:
            y_sum[row] += product(hidden[col], held[slot])
        else:
            turned = halves[index // half][index % half]
            x_sum[row] += product(acts[which * col_count + col], turned)

    def run(step, chosen):
        later = jnp.minimum(step + 1, steps - 1)
        for which, copy in enumerate(copies(later)):
            if which in chosen:
                pl.when(step + 1 < filled[which])(copy.wait)
        for index in range(slots):
            for which in chosen:
                multiply(which, step, index)
                if which < 2 and index < half:
                    turn(which, step, index + half)
                elif which < 2:
                    turn(which, later, index - half)

    for copy in copies(0):
        copy.wait()
    for index in range(half):
        for which in (0, 1):
            turn(which, 0, index)
    every = jnp.minimum(jnp.minimum(*filled[:2]), filled[2])
    each(0, every, lambda step: run(step, (0, 1, 2)))
    for which in range(3):
        each(every, filled[which], lambda step, i=which: run(step, (i,)))
    height = outs[0].shape[0] // 2
    for piece, out in enumerate(outs):
        tokens = slice(piece * height, (piece + 1) * height)
        for row in range(row_count):
            columns = slice(row * 128, (row + 1) * 128)
            out[:height, columns] = y_sum[row, tokens].astype(out.dtype)
            out[height:, columns] = x_sum[row, tokens].astype(out.dtype)


def grads_kernel(grid, rows, hiddens, acts, arrive, gate_ids, up_ids, down_ids, *refs):
    lists, refs = refs[:3], refs[3:]
    row_count, col_count = grid
    gate_out, up_out, down_out, x, g, hidden, gate_act, up_act = refs[-13:-5]
    gate_buf, up_buf, down_buf, nothing, sems = refs[-5:]

    def joined(groups, index):
        return jnp.concatenate([refs[array][first + index] for array, first in groups], axis=0)

    slot_count = gate_buf.shape[0]
    slots = divisor_up_to(slot_count, SLOTS_PER_STEP)
    steps = slot_count // slots
    pairs = ((gate_buf, gate_out), (up_buf, up_out), (down_buf, down_out))

    def copy(which, step, empty=False):
        buf, out = pairs[which]
        chunk = pl.ds(step * slots, slots)
        source = nothing if empty else buf.at[chunk]
        return pltpu.make_async_copy(source, out.at[0, 0, chunk], sems.at[which, step])

    zero(nothing)
    arrive()
    filled = [filled_steps(ids, grid, steps) for ids in lists]
    for which in range(3):
        each(filled[which], steps, lambda step, i=which: copy(i, step, True).start())
    for row in range(row_count):
        x[row] = joined(rows, row).T
        g[row] = joined(rows, row_count + row)
    zero(x.at[row_count])
    zero(g.at[row_count])
    for col in range(col_count):
        hidden[col] = joined(hiddens, col).T
        gate_act[col] = joined(acts, col)
        up_act[col] = joined(acts, col_count + col)
    matrices = (
        (gate_ids, x, gate_act, gate_buf),
        (up_ids, x, up_act, up_buf),
        (down_ids, g, hidden, down_buf),
    )

    def run(step, chosen):
        for which in chosen:
            ids, model, act, buf = matrices[which]
            for index in range(slots):
                slot = step * slots + index
                row, col = place(ids[0, 0, slot], *grid)
                left, right = (act[col], model[row]) if which == 2 else (model[row], act[col])
                buf[slot] = product(left, right).astype(buf.dtype)
        for which in chosen:
            copy(which, step).start()

    every = jnp.minimum(jnp.minimum(*filled[:2]), filled[2])
    each(0, every, lambda step: run(step, (0, 1, 2)))
    for which in range(3):
        each(every, filled[which], lambda step, i=which: run(step, (i,)))
    for which in range(3):
        each(0, steps, lambda step, i=which: copy(i, step).wait())


def sent(value, axis, target):
    size = lax.axis_size(axis)
    return lax.ppermute(value, axis, [(i, target(i, size)) for i in range(size)])


def beyond(device, distance, size):
    return (device + distance) % size if size & (size - 1) else device ^ distance


def gathered(value, axis):
    size = lax.axis_size(axis)
    return [value] + [
        sent(value, axis, lambda i, n, d=d: beyond(i, d, n)) for d in range(1, size)
    ]


def across(value, distance):
    return sent(value, "replica", lambda i, n: i ^ distance)


def scattered(pieces, axis):
    size = lax.axis_size(axis)
    sign = -1 if size & (size - 1) else 1
    return [pieces[0]] + [
        sent(pieces[d], axis, lambda i, n, d=d: beyond(i, sign * d, n)) for d in range(1, size)
    ]


def on_device(tokens, out_grad, gate_blocks, up_blocks, down_blocks, gate_ids, up_ids, down_ids):
    slot_count, block = gate_blocks.shape[2], gate_blocks.shape[-1]
    tile, groups = lax.axis_size("tile"), lax.axis_size("replica")
    height = tokens.shape[0]
    group = height * tile
    row_count = tokens.shape[1] // block
    col_count = FF // tile // block
    grid = (row_count, col_count)
    bf16, f32 = jnp.bfloat16, jnp.float32
    shape = jax.ShapeDtypeStruct
    step_flops = 2 * slot_count * group * block * block

    token_parts, grad_parts = gathered(tokens, "tile"), gathered(out_grad, "tile")
    gate_up = call(
        functools.partial(gate_up_kernel, grid),
        shape((2, col_count, group, block), bf16),
        [gate_ids, up_ids, gate_ids, up_ids, *token_parts, gate_blocks, up_blocks],
        2,
        [pltpu.VMEM((row_count + 1, group, block), bf16)]
        + [pltpu.VMEM((col_count, group, block), f32)] * 2
        + stream_scratch(gate_blocks, 2, limit=48),
        48,
        2 * step_flops,
        fetched=3,
    )
    _, grad_parts = lax.optimization_barrier((gate_up, grad_parts))
    rows = call(
        functools.partial(rows_kernel, row_count),
        shape((2 * row_count + 1, group, block), bf16),
        [*token_parts, *grad_parts],
        0,
        [],
        8,
        1,
    )
    packed = groups == 4
    far_rows = across(rows, 2) if packed else None
    back = call(
        functools.partial(back_kernel, grid),
        shape((col_count, group, block), bf16),
        [down_ids, rows, down_blocks],
        1,
        [
            pltpu.VMEM((col_count, group, block), f32),
            *turned_scratch(down_blocks, 1),
            *stream_scratch(down_blocks, 1, 2),
        ],
        48,
        step_flops,
    )
    gate_up_parts = gathered(gate_up, "dp")
    gate_up_parts, _ = lax.optimization_barrier((gate_up_parts, back))
    hidden = call(
        functools.partial(hidden_kernel, col_count),
        shape((col_count, group, block), bf16),
        gate_up_parts,
        0,
        [],
        8,
        1,
    )
    far_hidden = across(hidden, 2) if packed else None
    back_parts, far_rows, hidden = lax.optimization_barrier(
        (gathered(back, "dp"), far_rows, hidden)
    )
    acts_shape = shape((2 * col_count, group, block), bf16)
    row_blocks = 2 * row_count
    pack_shape = shape((2 * row_blocks + 3 * col_count, group, block), bf16)
    acts, *pack = call(
        functools.partial(act_grads_kernel, col_count, len(back_parts), 2 * packed, row_blocks),
        [acts_shape, pack_shape] if packed else [acts_shape],
        [*gate_up_parts, *back_parts, hidden, *([rows, far_rows] if packed else [])],
        0,
        [],
        8,
        1,
    )
    far_acts = across(acts, 2) if packed else None
    pieces = call(
        functools.partial(model_kernel, grid),
        [shape((2 * height, row_count * block), bf16)] * tile,
        [
            *[gate_ids, up_ids, down_ids] * 2,
            hidden,
            acts,
            gate_blocks,
            up_blocks,
            down_blocks,
        ],
        3,
        [pltpu.VMEM((row_count + 1, group, block), f32)] * 2
        + [*turned_scratch(gate_blocks, 2, 2), *stream_scratch(gate_blocks, 3)],
        48,
        3 * step_flops,
        fetched=3,
    )
    if packed:
        _, far_hidden, far_acts = lax.optimization_barrier((pieces, far_hidden, far_acts))
        arrays = [rows, far_rows, across(pack[0], 1), hidden, far_hidden, across(far_hidden, 1)]
        arrays += [acts, far_acts, across(far_acts, 1)]
        rows_at = ((0, 0), (1, 0), (2, 0), (2, row_blocks))
        hidden_at = ((3, 0), (4, 0), (2, 2 * row_blocks), (5, 0))
        acts_at = ((6, 0), (7, 0), (2, 2 * row_blocks + col_count), (8, 0))
    else:
        arrays = [piece for whole in (rows, hidden, acts) for piece in gathered(whole, "replica")]
        rows_at, hidden_at, acts_at = (
            tuple((first * groups + i, 0) for i in range(groups)) for first in range(3)
        )
    total = group * groups
    slots = divisor_up_to(slot_count, SLOTS_PER_STEP)
    grads = call(
        functools.partial(grads_kernel, grid, rows_at, hidden_at, acts_at),
        [shape(gate_blocks.shape, bf16)] * 3,
        [gate_ids, up_ids, down_ids, gate_ids, up_ids, down_ids, *arrays],
        3,
        [
            pltpu.VMEM((row_count + 1, block, total), bf16),
            pltpu.VMEM((row_count + 1, total, block), bf16),
            pltpu.VMEM((col_count, block, total), bf16),
            pltpu.VMEM((col_count, total, block), bf16),
            pltpu.VMEM((col_count, total, block), bf16),
        ]
        + [pltpu.VMEM((slot_count, block, block), bf16)] * 3
        + [
            pltpu.VMEM((slots, block, block), bf16),
            pltpu.SemaphoreType.DMA((3, slot_count // slots)),
        ],
        46,
        3 * step_flops * groups,
        out_hbm=True,
        fetched=3,
    )
    pieces, grads = lax.optimization_barrier((scattered(pieces, "tile"), grads))
    output, input_grad = (
        sum(piece[half].astype(f32) for piece in pieces).astype(bf16)
        for half in (slice(height), slice(height, None))
    )
    return (output, input_grad, *grads)


def solution(mesh):
    rows = P(("tile", "replica"), "dp")
    blocks = P("dp", "tile", None, None, None)
    ids = P("dp", "tile", None)
    return jax.shard_map(
        on_device,
        mesh=mesh,
        in_specs=(rows, rows, blocks, blocks, blocks, ids, ids, ids),
        out_specs=(rows, rows, blocks, blocks, blocks),
        check_vma=False,
    )
```
